32 devices in a mesh: parts: 2 (over y), bank: 4 (over z), tm: 2 (over x), rate: 2 (over core).
Axes of the slice: x: 2, y: 2, z: 4, core: 2. Of those that a mesh axis runs over, the one named last changes fastest.
Arguments:
- strain: float32 [2, 16384], P('rate', ('parts', 'bank', 'tm')), parts along dimension 1, may hold values from -6 to 6
- gate_mask: int32 [16384], P(('parts', 'bank', 'tm')), parts along dimension 0, may hold values 0 or 1
- psd_reset: int32 [16], P(('parts', 'bank', 'tm')), parts along dimension 0, may hold values from 0 to 1
- psd_ref: float32 [2, 512], P('rate'), may hold values from 0.1 to 10
- psd_rate: float32 [2, 512], P('rate'), may hold values from 0.025 to 0.5
- filters: bfloat16 [4, 2, 32, 2048], P('bank', 'rate'), may hold values from -0.125 to 0.125
- basis_count: int32 [4], P('bank'), may hold values from 16 to 32, as said below
- mixing: bfloat16 [4, 2, 4, 2, 32], P('bank', 'rate'), may hold values from -0.75 to 0.75
- autocorrelation: float32 [4, 2, 257], replicated, may hold values from -1.2 to 1.2
Outputs:
- snr_sq: float32 [4, 4, 16384], P(None, 'rate', ('parts', 'bank', 'tm')), parts along dimension 2
- chisq: float32 [4, 4, 16384], P(None, 'rate', ('parts', 'bank', 'tm')), parts along dimension 2
The draws below stay inside these ranges and needn't reach their ends.
There are 2 independent parts, one for each index of `parts`. The reference program is written for one: setup_inputs(seed, part) draws one part's arguments, and reference() takes and returns one part's arrays. A program takes and returns all parts, laid end to end along the dimension named above; an argument that names none is the same for every part. Nothing has to cross between parts.
Inputs may be any that keep to these rules, and one draw needn't show every extreme that they name: `basis_count`: some bank uses all 32 basis filters and another only half of them.
All inputs are finite; a program needn't handle non-finite values. No bound on the sum of `gate_mask` on one device may be relied on, other than what follows from the above.
Results may differ from the reference program's by a relative error of at most 0.0044.
Values may be sent and summed in bfloat16 or wider, within the bound.
No kernel may reach another device: no remote copies, remote signals or barrier semaphores. Data moves between devices by JAX's collectives and lax.ppermute only.
A program may use at most 128 MiB of HBM per device.

```python
import math
import jax
import jax.numpy as jnp
from jax import lax

PIECE = 1024
TAPS = 2048
BASIS = 32
TEMPL = 4
ACL_HALF = 128
BANKS = 4
BANDS = 2
PIECES = 8
TIME = 8192
BINS = 512
ACL = 257


def draw_basis_count(key, part):
    key_one = jax.random.fold_in(key, 11)
    key_two = jax.random.fold_in(key, 12)
    key_three = jax.random.fold_in(key, 13)
    counts = jax.random.randint(key_one, (BANKS,), BASIS // 2, BASIS + 1)
    top_bank = jax.random.randint(key_two, (), 0, BANKS)
    low_bank = (top_bank + 1 + jax.random.randint(key_three, (), 0, BANKS - 1)) % BANKS
    positions = jnp.arange(BANKS)
    counts = jnp.where(positions == top_bank, BASIS, counts)
    counts = jnp.where(positions == low_bank, BASIS // 2, counts)
    return counts.astype(jnp.int32)


def draw_psd_reset(key, part):
    key_one = jax.random.fold_in(key, 21)
    rolls = jax.random.randint(key_one, (PIECES,), 0, 8)
    resets = jnp.where(rolls == 0, 1, 0)
    positions = jnp.arange(PIECES)
    first_block = part % PIECES
    second_block = (part + 1) % PIECES
    resets = jnp.where(positions == first_block, 1, resets)
    resets = jnp.where(positions == second_block, 0, resets)
    return resets.astype(jnp.int32)


def touch_ends(values, stream_key, low, top_value):
    spot = [jax.random.randint(jax.random.fold_in(stream_key, axis), (), 0, length) for axis, length in enumerate(values.shape)]
    widest = values.shape.index(max(values.shape))
    next_to = spot[:widest] + [(spot[widest] + 1) % values.shape[widest]] + spot[widest + 1:]
    return values.at[tuple(spot)].set(low).at[tuple(next_to)].set(top_value)


def block_levels(rng, extent, pieces, least, high):
    loudness, own = 1.0, jax.random.fold_in(rng, 6)
    for dim, parts in pieces:
        draws = jnp.exp(jax.random.uniform(jax.random.fold_in(own, dim), (parts,), jnp.float32, least / len(pieces), high / len(pieces)))
        loudness = loudness * jnp.repeat(draws, extent[dim] // parts).reshape([-1 if axis == dim else 1 for axis in range(len(extent))])
    return loudness


def normal_values(stream_key, extent, deviation, reach, split=(), kind=jnp.bfloat16):
    result = jax.random.normal(stream_key, extent, jnp.float32) * deviation
    if len(split) > 0:
        result = block_levels(stream_key, extent, split, -0.22, 0.18) * result
    return jnp.clip(result, min=-reach, max=reach).astype(kind)


def setup_inputs(seed: int = 0, part: int = 0) -> dict:
    splits = jax.random.split(jax.random.key(seed), 10)
    part_splits = jax.random.split(jax.random.fold_in(splits[9], part), 10)
    return {
        "strain": normal_values(part_splits[0], (BANDS, TIME), 1.0, 6.0, ((0, 2), (1, 8)), jnp.float32),
        "gate_mask": touch_ends((jax.random.randint(part_splits[1], (TIME,), 0, 32) < 31).astype(jnp.int32), jax.random.fold_in(part_splits[1], 1), 0, 1),
        "psd_reset": draw_psd_reset(jax.random.fold_in(jax.random.fold_in(splits[9], part), 71), part),
        "psd_ref": jnp.clip(jnp.exp(math.log(10.0) - 4.6051702 * jax.random.uniform(splits[3], (BANDS, BINS), jnp.float32) ** block_levels(splits[3], (BANDS, BINS), ((0, 2),), -0.2, 0.2)), 0.1, 10.0),
        "psd_rate": jnp.clip(jnp.exp(math.log(0.5) - 2.9957323 * jax.random.uniform(splits[4], (BANDS, BINS), jnp.float32) ** block_levels(splits[4], (BANDS, BINS), ((0, 2),), -0.2, 0.2)), 0.025, 0.5),
        "filters": normal_values(splits[5], (BANKS, BANDS, BASIS, TAPS), TAPS ** -0.5, 0.125, ((0, 4), (1, 2))),
        "basis_count": draw_basis_count(jax.random.fold_in(splits[9], 71), part),
        "mixing": normal_values(splits[7], (BANKS, BANDS, TEMPL, 2, BASIS), (2 * BASIS) ** -0.5, 0.75, ((0, 4), (1, 2))),
        "autocorrelation": normal_values(splits[8], (BANKS, 2, ACL), 0.3, 1.2, (), jnp.float32),
    }


HIGHEST = lax.Precision.HIGHEST


def dft_tables(length):
    bin_count = length // 2
    sample = jnp.arange(length, dtype=jnp.int32)
    frequency = jnp.arange(bin_count, dtype=jnp.int32)
    phase_index = (sample[:, None] * frequency[None, :]) % length
    angle_value = phase_index.astype(jnp.float32) * (2.0 * math.pi / length)
    weights = jnp.where(frequency == 0, 1.0 / length, 2.0 / length).astype(jnp.float32)
    return jnp.cos(angle_value), jnp.sin(angle_value), weights


def reference(strain, gate_mask, psd_reset, psd_ref, psd_rate, filters, basis_count, mixing, autocorrelation):
    cos_table, sin_table, weights = dft_tables(PIECE)
    gated = strain * gate_mask.astype(jnp.float32)[None, :]
    blocks = gated.reshape(BANDS, PIECES, PIECE)
    real_part = jnp.einsum('cgn,nk->cgk', blocks, cos_table, precision=HIGHEST)
    imag_part = jnp.einsum('cgn,nk->cgk', blocks, sin_table, precision=HIGHEST)
    log_power = jnp.log((real_part * real_part + imag_part * imag_part) / (PIECE / 2) + 0.1 * psd_ref[:, None, :])
    keep_factor = (1.0 - psd_rate)[:, None, :] * (1.0 - 0.5 * psd_reset.astype(jnp.float32))[None, :, None]
    drive_term = psd_rate[:, None, :] * log_power

    def advance(state_now, inputs):
        keep_now, drive_now = inputs
        state_next = keep_now * state_now + drive_now
        return state_next, state_next

    final_state, log_psd = lax.scan(advance, jnp.log(psd_ref), (keep_factor.transpose(1, 0, 2), drive_term.transpose(1, 0, 2)))
    log_psd = log_psd.transpose(1, 0, 2)
    bin_scale = jnp.exp(-0.5 * log_psd) * weights
    whitened = jnp.einsum('cgk,nk->cgn', real_part * bin_scale, cos_table, precision=HIGHEST)
    whitened = whitened + jnp.einsum('cgk,nk->cgn', imag_part * bin_scale, sin_table, precision=HIGHEST)
    whitened = whitened.reshape(BANDS, TIME).astype(jnp.bfloat16)

    fft_length = 2 ** int(math.ceil(math.log2(TIME + TAPS + 2 * ACL_HALF + 1)))
    spec_strain = jnp.fft.rfft(whitened.astype(jnp.float32), fft_length)
    ones_kernel = jnp.ones((ACL,), jnp.float32)
    ones_spec = jnp.fft.rfft(ones_kernel, fft_length)

    def per_bank(inputs):
        taps_bank, count_bank, mixing_bank, series_bank = inputs
        spec_taps = jnp.fft.rfft(taps_bank.astype(jnp.float32), fft_length)
        outputs = jnp.fft.irfft(spec_taps * spec_strain[:, None, :], fft_length)[..., :TIME]
        live_basis = (jnp.arange(BASIS, dtype=jnp.int32) < count_bank).astype(jnp.float32)
        basis = (outputs * live_basis[None, :, None]).astype(jnp.bfloat16)
        snr = jnp.einsum('cmpi,cit->mpt', mixing_bank.astype(jnp.float32), basis.astype(jnp.float32))
        energy = snr[:, 0] * snr[:, 0] + snr[:, 1] * snr[:, 1]
        complex_snr = snr[:, 0] + 1j * snr[:, 1]
        kernel = jnp.conj(series_bank[0] + 1j * series_bank[1])[::-1]
        folded = jnp.fft.ifft(jnp.fft.fft(complex_snr, fft_length) * jnp.fft.fft(kernel, fft_length))
        folded = folded[:, ACL_HALF:ACL_HALF + TIME]
        window_sum = jnp.fft.irfft(jnp.fft.rfft(energy, fft_length) * ones_spec, fft_length)[:, ACL_HALF:ACL_HALF + TIME]
        lag_energy = jnp.sum(series_bank * series_bank)
        cross = snr[:, 0] * jnp.real(folded) + snr[:, 1] * jnp.imag(folded)
        chisq = (window_sum - 2.0 * cross + energy * lag_energy) / ACL
        return energy, chisq

    snr_sq, chisq = lax.map(per_bank, (filters, basis_count, mixing, autocorrelation))
    return snr_sq, chisq
```

```python
import functools
import math

import jax
import jax.numpy as jnp
import numpy as np
from jax import lax
from jax.experimental import pallas as pl
from jax.experimental.pallas import tpu as pltpu
from jax.sharding import PartitionSpec as P

HIGHEST = lax.Precision.HIGHEST
LANES = 128
F32 = jnp.float32
BF16 = jnp.bfloat16


def swapped(block, axis, distance):
    route = [(i, i ^ distance) for i in range(lax.axis_size(axis))]
    return lax.ppermute(block, axis, route)


def tables(length):
    rows = length // LANES
    high = length // 2 // LANES
    lane = np.arange(LANES)
    turn = 2.0 * math.pi
    outer = turn * (np.arange(rows)[:, None] * lane[None, :] % rows) / rows
    outer = np.stack([np.cos(outer), np.sin(outer)])
    inner = turn * (lane[:, None] * lane[None, :]) / length
    inner = np.concatenate([np.cos(inner), np.sin(inner)], axis=1)
    shift = turn * (np.arange(high)[:, None] * lane[None, :] % rows) / rows
    shift = np.stack([np.cos(shift), np.sin(shift)])
    bins = np.arange(length // 2)
    full = turn * (bins[:, None] * lane[None, :] % length) / length
    full = np.concatenate([np.cos(full), np.sin(full)], axis=0)
    weight = np.where(bins == 0, 1.0 / length, 2.0 / length).reshape(high, LANES)
    return tuple(a.astype(np.float32) for a in (outer, inner, shift, full, weight))


def split_two(value):
    upper = value.astype(BF16)
    return upper, (value - upper.astype(F32)).astype(BF16)


def circulant(row):
    spread = jnp.broadcast_to(row, (LANES, LANES))
    return pltpu.roll(spread, 0, 1, stride=1, stride_axis=0)


def keep_right():
    u = lax.broadcasted_iota(jnp.int32, (LANES, LANES), 0)
    q = lax.broadcasted_iota(jnp.int32, (LANES, LANES), 1)
    return q >= u


def spectrum_kernel(strain, mask, reset, psd_ref, psd_rate, outer, inner, shift, out):
    rows = strain.shape[0]
    high = psd_ref.shape[0]
    signal = strain[...] * mask[...].astype(F32)
    left = []
    for part in range(2):
        for kh in range(high):
            left.append(signal * shift[part, kh : kh + 1, :])
    product = lax.dot_general(
        jnp.concatenate(left, axis=0),
        inner[...],
        (((1,), (0,)), ((), ())),
        precision=HIGHEST,
        preferred_element_type=F32,
    )
    cos_one, sin_one = outer[0], outer[1]
    real_rows, imag_rows = [], []
    for kh in range(high):
        with_cos = product[kh * rows : (kh + 1) * rows]
        with_sin = product[(high + kh) * rows : (high + kh + 1) * rows]
        cos_sum = with_cos[:, :LANES] - with_sin[:, LANES:]
        sin_sum = with_cos[:, LANES:] + with_sin[:, :LANES]
        real_rows.append(jnp.sum(cos_one * cos_sum - sin_one * sin_sum, axis=0, keepdims=True))
        imag_rows.append(jnp.sum(sin_one * cos_sum + cos_one * sin_sum, axis=0, keepdims=True))
    real_part = jnp.concatenate(real_rows, axis=0)
    imag_part = jnp.concatenate(imag_rows, axis=0)
    reference_psd = psd_ref[...]
    rate = psd_rate[...]
    power = (real_part * real_part + imag_part * imag_part) / (rows * LANES / 2)
    log_power = jnp.log(power + 0.1 * reference_psd)
    keep = (1.0 - rate) * (1.0 - 0.5 * reset[0].astype(F32))
    first = (lax.axis_index("bank") == 0) & (lax.axis_index("tm") == 0)
    drive = rate * log_power + jnp.where(first, keep * jnp.log(reference_psd), 0.0)
    whole = jnp.concatenate([real_part, imag_part, drive, keep], axis=0)
    upper, lower = split_two(whole)
    out[: 4 * high] = upper
    out[4 * high :] = lower


def filter_kernel(filters, mixing, count, out):
    total, basis = mixing.shape
    share = total // 2
    templ = share // 2
    rate = lax.axis_index("rate")
    row = lax.broadcasted_iota(jnp.int32, (total, total), 0)
    col = lax.broadcasted_iota(jnp.int32, (total, total), 1)
    part = (row // share) ^ rate
    source = (part * templ + row % templ) * 2 + row % share // templ
    choose = (col == source).astype(BF16)
    ordered = jnp.dot(choose, mixing[...], preferred_element_type=F32)
    live = lax.broadcasted_iota(jnp.int32, (total, basis), 1) < count[0]
    ordered = jnp.where(live, ordered, 0.0).astype(BF16)
    combined = jnp.dot(ordered, filters[...], preferred_element_type=F32)
    lags = filters.shape[1] // LANES
    low_half = lax.broadcasted_iota(jnp.int32, (total, LANES), 0) < share
    own, other = [], []
    for a in range(0, lags, 2):
        even = combined[:, a * LANES : (a + 1) * LANES]
        odd = combined[:, (a + 1) * LANES : (a + 2) * LANES]
        own.append(jnp.where(low_half, even, pltpu.roll(odd, share, 0)))
        other.append(jnp.where(low_half, pltpu.roll(even, share, 0), odd))
    out[...] = jnp.concatenate(own + other, axis=0).astype(BF16)


def band_kernel(series, upper_out, lower_out, lag_out):
    right = keep_right()
    for b in range(series.shape[0]):
        lag = jnp.zeros((1, 1), F32)
        for part in range(2):
            row = series[b, part : part + 1, :]
            lag = lag + jnp.sum(row * row, axis=1, keepdims=True)
            before = jnp.zeros((LANES, LANES), F32)
            for d in range(3):
                now = circulant(row[:, d * LANES : (d + 1) * LANES])
                upper, lower = split_two(jnp.where(right, now, before))
                upper_out[b, part * LANES : (part + 1) * LANES, d * LANES : (d + 1) * LANES] = upper
                lower_out[b, part * LANES : (part + 1) * LANES, d * LANES : (d + 1) * LANES] = lower
                before = now
        lag_out[b] = jnp.broadcast_to(lag, (8, LANES))


def output_kernel(
    own_a, own_b, other_a, other_b, full, outer, weight, band_up, band_low, lag,
    snr_out, chi_out, spec, logs, toeplitz, *, banks, tms, length, taps, window,
):
    rows = length // LANES
    high = length // 2 // LANES
    spec_rows = 8 * high
    lags = taps // LANES
    lag_rows = lags * 4
    piece_rows = tms * spec_rows + 2 * lag_rows
    pieces = banks * tms
    behind = -(-(taps + window) // length)
    near = behind + 2
    half = max(banks // 2, 1)
    bank = lax.axis_index("bank")
    tm = lax.axis_index("tm")
    place = bank * tms + tm
    bufs = ((own_a, own_b), (other_a, other_b))

    def piece(c, d):
        return bufs[c][d // half], (d % half) * piece_rows

    zero = jnp.zeros((4 * high, LANES), F32)
    for c in range(2):
        for i in range(behind):
            spec[c, i] = zero
            logs[c, i] = zero[:high]
        spec[c, pieces + behind] = zero
        logs[c, pieces + behind] = zero[:high]
        for d in range(banks):
            ref, start = piece(c, d)
            for e in range(tms):
                top = start + e * spec_rows
                value = ref[top : top + 4 * high].astype(F32)
                value = value + ref[top + 4 * high : top + 8 * high].astype(F32)
                spec[c, ((bank ^ d) * tms + (tm ^ e)) + behind] = value

    def advance(g, states):
        nexts = []
        for c in range(2):
            drive = spec[c, g + behind, 2 * high : 3 * high]
            keep = spec[c, g + behind, 3 * high : 4 * high]
            nexts.append(keep * states[c] + drive)
            logs[c, g + behind] = nexts[c]
        return tuple(nexts)

    states = (zero[:high], zero[:high])
    if pieces <= 16:
        for g in range(pieces):
            states = advance(g, states)
    else:
        lax.fori_loop(0, pieces, advance, states)

    cos_one, sin_one = outer[0], outer[1]
    left = []
    for c in range(2):
        for i in range(near):
            scale = jnp.exp(-0.5 * logs[c, place + i]) * weight[...]
            real = spec[c, place + i, :high] * scale
            imag = spec[c, place + i, high : 2 * high] * scale
            cos_parts, sin_parts = [], []
            for kh in range(high):
                re = jnp.broadcast_to(real[kh : kh + 1], (rows, LANES))
                im = jnp.broadcast_to(imag[kh : kh + 1], (rows, LANES))
                cos_parts.append(re * cos_one + im * sin_one)
                sin_parts.append(im * cos_one - re * sin_one)
            left.append(jnp.concatenate(cos_parts + sin_parts, axis=1))
    white = lax.dot_general(
        jnp.concatenate(left, axis=0),
        full[...],
        (((1,), (0,)), ((), ())),
        precision=HIGHEST,
        preferred_element_type=F32,
    )
    white = white.astype(BF16).astype(F32)

    first_out = behind * rows - 1
    out_frames = rows + 2
    first_t = first_out - (lags - 1)
    t_frames = lags - 1 + out_frames
    right = keep_right()
    for c in range(2):
        base = c * near * rows
        before = circulant(white[base + first_t - 1 : base + first_t])
        for s in range(t_frames):
            at = base + first_t + s
            now = circulant(white[at : at + 1])
            toeplitz[c * LANES : (c + 1) * LANES, s * LANES : (s + 1) * LANES] = jnp.where(
                right, now, before
            ).astype(BF16)
            before = now

    low_half = lax.broadcasted_iota(jnp.int32, (8, LANES), 0) < 4
    low_phase = lax.broadcasted_iota(jnp.int32, (8, LANES), 0) % 4 < 2
    after = jnp.where(place == pieces - 1, 0.0, 1.0).astype(F32)
    lane_row = lax.broadcasted_iota(jnp.int32, (LANES, LANES), 0)
    lane_col = lax.broadcasted_iota(jnp.int32, (LANES, LANES), 1)
    upto = (lane_row <= lane_col).astype(BF16)
    sums = jnp.concatenate([upto, jnp.ones((LANES, LANES), BF16)], axis=1)

    def conv(d):
        parts = []
        for c in range(2):
            ref, start = piece(c, d)
            top = start + tms * spec_rows + c * lag_rows
            parts.append(ref[top : top + lag_rows])
        return jnp.concatenate(parts, axis=1)

    def frames_of(g_all, row):
        accs = []
        for n in range(out_frames + 1):
            acc = None
            for a in range(lags // 2):
                s = n - 1 + (lags - 1) - 2 * a
                if 0 <= s < t_frames:
                    tile = g_all[row + 8 * a : row + 8 * a + 8, s * LANES : (s + 1) * LANES]
                    acc = tile if acc is None else acc + tile
            accs.append(acc)
        return [accs[n + 1] + pltpu.roll(accs[n], 4, 0) for n in range(out_frames)]

    for group in range(0, banks, 4):
        members = range(group, min(group + 4, banks))
        f_all = jnp.concatenate([conv(d) for d in members], axis=0)
        g_all = jnp.dot(f_all, toeplitz[...], preferred_element_type=F32)
        for first in range(0, len(members), 2):
            d0, d1 = members[first], members[first + 1]
            z0 = frames_of(g_all, first * lag_rows)
            z1 = frames_of(g_all, (first + 1) * lag_rows)
            z = [jnp.where(low_half, p, pltpu.roll(q, 4, 0)) for p, q in zip(z0, z1)]
            z[-1] = z[-1] * after
            stacked = jnp.concatenate(
                [jnp.concatenate(z[n : n + rows], axis=0) for n in range(3)], axis=1
            )
            up, low = split_two(stacked)
            corr = []
            for d in (d0, d1):
                b_up = band_up[bank ^ d]
                b_low = band_low[bank ^ d]
                dims = (((1,), (1,)), ((), ()))
                corr.append(
                    lax.dot_general(up, b_up, dims, preferred_element_type=F32)
                    + lax.dot_general(low, b_up, dims, preferred_element_type=F32)
                    + lax.dot_general(up, b_low, dims, preferred_element_type=F32)
                )
            power = []
            for v in z:
                square = v * v
                power.append(square + pltpu.roll(square, 6, 0))
            p_up, p_low = split_two(jnp.concatenate(power, axis=0))
            run = jnp.dot(p_up, sums, preferred_element_type=F32) + jnp.dot(
                p_low, sums, preferred_element_type=F32
            )
            lag_now = jnp.where(low_half, lag[bank ^ d0], lag[bank ^ d1])
            for n in range(rows):
                tile = slice(8 * n, 8 * n + 8)
                c_re = jnp.where(low_half, corr[0][tile, :LANES], corr[1][tile, :LANES])
                c_im = jnp.where(low_half, corr[0][tile, LANES:], corr[1][tile, LANES:])
                mid = z[n + 1]
                turned = jnp.where(low_phase, -pltpu.roll(mid, 6, 0), pltpu.roll(mid, 2, 0))
                cross = mid * c_re + turned * c_im
                cross = cross + pltpu.roll(cross, 6, 0)
                prev = slice(8 * n, 8 * n + 8)
                here = slice(8 * n + 8, 8 * n + 16)
                nxt = slice(8 * n + 16, 8 * n + 24)
                win = (run[prev, LANES:] - run[prev, :LANES] + power[n]) + (
                    run[here, LANES:] + run[nxt, :LANES]
                )
                energy = power[n + 1]
                chi = (win - 2.0 * cross + energy * lag_now) / (2 * window + 1)
                lanes = slice(n * LANES, (n + 1) * LANES)
                snr_out[bank ^ d0, :, lanes] = energy[0:2]
                snr_out[bank ^ d1, :, lanes] = energy[4:6]
                chi_out[bank ^ d0, :, lanes] = chi[0:2]
                chi_out[bank ^ d1, :, lanes] = chi[4:6]


VMEM = pl.BlockSpec(memory_space=pltpu.VMEM)
SMEM = pl.BlockSpec(memory_space=pltpu.SMEM)


def body(
    strain, gate_mask, psd_reset, psd_ref, psd_rate, filters, basis_count, mixing, autocorrelation
):
    length = strain.shape[1]
    rows = length // LANES
    high = length // 2 // LANES
    banks = lax.axis_size("bank")
    tms = lax.axis_size("tm")
    basis, taps = filters.shape[2:]
    templ = mixing.shape[2]
    window = autocorrelation.shape[2] // 2
    lags = taps // LANES
    outer, inner, shift, full, weight = tables(length)

    spec = pl.pallas_call(
        spectrum_kernel,
        out_shape=jax.ShapeDtypeStruct((8 * high, LANES), BF16),
        in_specs=[VMEM, VMEM, SMEM] + [VMEM] * 5,
        out_specs=VMEM,
        name="spectrum",
    )(
        strain.reshape(rows, LANES),
        gate_mask.reshape(rows, LANES),
        psd_reset,
        psd_ref.reshape(high, LANES),
        psd_rate.reshape(high, LANES),
        outer,
        inner,
        shift,
    )
    combined = pl.pallas_call(
        filter_kernel,
        out_shape=jax.ShapeDtypeStruct((2 * templ * lags, LANES), BF16),
        in_specs=[VMEM, VMEM, SMEM],
        out_specs=VMEM,
        name="filters",
    )(filters.reshape(basis, taps), mixing.reshape(2 * templ, basis), basis_count)
    padded = jnp.pad(autocorrelation, ((0, 0), (0, 0), (0, 3 * LANES - 2 * window - 1)))
    band = jax.ShapeDtypeStruct((banks, 2 * LANES, 3 * LANES), BF16)
    band_up, band_low, lag = pl.pallas_call(
        band_kernel,
        out_shape=(band, band, jax.ShapeDtypeStruct((banks, 8, LANES), F32)),
        in_specs=[VMEM],
        out_specs=(VMEM, VMEM, VMEM),
        name="bands",
    )(padded)

    distance = 1
    while distance < tms:
        spec = jnp.concatenate([spec, swapped(spec, "tm", distance)])
        distance *= 2
    held = jnp.concatenate([spec, combined])
    distance = 1
    while distance * 2 < banks:
        held = jnp.concatenate([held, swapped(held, "bank", distance)])
        distance *= 2
    far = swapped(held, "bank", distance)
    held_other = swapped(held, "rate", 1)
    far_other = swapped(far, "rate", 1)

    behind = -(-(taps + window) // length)
    near = behind + 2
    share = templ // 2
    out = jax.ShapeDtypeStruct((banks, share, length), F32)
    return pl.pallas_call(
        functools.partial(
            output_kernel, banks=banks, tms=tms, length=length, taps=taps, window=window
        ),
        out_shape=(out, out),
        in_specs=[VMEM] * 10,
        out_specs=(VMEM, VMEM),
        scratch_shapes=[
            pltpu.VMEM((2, banks * tms + behind + 1, 4 * high, LANES), F32),
            pltpu.VMEM((2, banks * tms + behind + 1, high, LANES), F32),
            pltpu.VMEM((2 * LANES, (lags + rows + 1) * LANES), BF16),
        ],
        name="outputs",
    )(held, far, held_other, far_other, full, outer, weight, band_up, band_low, lag)


def solution(mesh):
    return jax.shard_map(
        body,
        mesh=mesh,
        in_specs=(
            P("rate", ("parts", "bank", "tm")),
            P(("parts", "bank", "tm")),
            P(("parts", "bank", "tm")),
            P("rate", None),
            P("rate", None),
            P("bank", "rate", None, None),
            P("bank"),
            P("bank", "rate", None, None, None),
            P(),
        ),
        out_specs=(
            P(None, "rate", ("parts", "bank", "tm")),
            P(None, "rate", ("parts", "bank", "tm")),
        ),
        check_vma=False,
    )
```

```python
import functools
import math

import jax
import jax.numpy as jnp
import numpy as np
from jax import lax
from jax.experimental import pallas as pl
from jax.experimental.pallas import tpu as pltpu
from jax.sharding import PartitionSpec as P


HIGHEST = lax.Precision.HIGHEST
LANES = 128
F32 = jnp.float32
BF16 = jnp.bfloat16


def swapped(block, axis, distance):
    route = [(i, i ^ distance) for i in range(lax.axis_size(axis))]
    return lax.ppermute(block, axis, route)


def tables(length):
    rows = length // LANES
    high = length // 2 // LANES
    lane = np.arange(LANES)
    turn = 2.0 * math.pi
    outer = turn * (np.arange(rows)[:, None] * lane[None, :] % rows) / rows
    outer = np.stack([np.cos(outer), np.sin(outer)])
    inner = turn * (lane[:, None] * lane[None, :]) / length
    inner = np.concatenate([np.cos(inner), np.sin(inner)], axis=1)
    shift = turn * (np.arange(high)[:, None] * lane[None, :] % rows) / rows
    shift = np.stack([np.cos(shift), np.sin(shift)])
    bins = np.arange(length // 2)
    full = turn * (bins[:, None] * lane[None, :] % length) / length
    full = np.concatenate([np.cos(full), np.sin(full)], axis=0)
    return tuple(a.astype(np.float32) for a in (outer, inner, shift, full))


def split_two(value):
    upper = value.astype(BF16)
    return upper, (value - upper.astype(F32)).astype(BF16)


def circulant(row):
    spread = jnp.broadcast_to(row, (LANES, LANES))
    return pltpu.roll(spread, 0, 1, stride=1, stride_axis=0)


def keep_right():
    u = lax.broadcasted_iota(jnp.int32, (LANES, LANES), 0)
    q = lax.broadcasted_iota(jnp.int32, (LANES, LANES), 1)
    return q >= u


def spectrum_kernel(strain, mask, reset, psd_ref, psd_rate, outer, inner, shift, out):
    rows = strain.shape[0]
    high = psd_ref.shape[0]
    signal = strain[...] * mask[...].astype(F32)
    left = []
    for part in range(2):
        for kh in range(high):
            left.append(signal * shift[part, kh : kh + 1, :])
    product = lax.dot_general(
        jnp.concatenate(left, axis=0),
        inner[...],
        (((1,), (0,)), ((), ())),
        precision=HIGHEST,
        preferred_element_type=F32,
    )
    cos_one, sin_one = outer[0], outer[1]
    real_rows, imag_rows = [], []
    for kh in range(high):
        with_cos = product[kh * rows : (kh + 1) * rows]
        with_sin = product[(high + kh) * rows : (high + kh + 1) * rows]
        cos_sum = with_cos[:, :LANES] - with_sin[:, LANES:]
        sin_sum = with_cos[:, LANES:] + with_sin[:, :LANES]
        real_rows.append(jnp.sum(cos_one * cos_sum - sin_one * sin_sum, axis=0, keepdims=True))
        imag_rows.append(jnp.sum(sin_one * cos_sum + cos_one * sin_sum, axis=0, keepdims=True))
    real_part = jnp.concatenate(real_rows, axis=0)
    imag_part = jnp.concatenate(imag_rows, axis=0)
    reference_psd = psd_ref[...]
    rate = psd_rate[...]
    power = (real_part * real_part + imag_part * imag_part) / (rows * LANES / 2)
    log_power = jnp.log(power + 0.1 * reference_psd)
    keep = (1.0 - rate) * (1.0 - 0.5 * reset[0].astype(F32))
    first = (lax.axis_index("bank") == 0) & (lax.axis_index("tm") == 0)
    drive = rate * log_power + jnp.where(first, keep * jnp.log(reference_psd), 0.0)
    whole = jnp.concatenate([real_part, imag_part, drive, keep], axis=0)
    upper, lower = split_two(whole)
    out[: 4 * high] = upper
    out[4 * high :] = lower


def filter_kernel(filters, mixing, count, out):
    total, basis = mixing.shape
    share = total // 2
    templ = share // 2
    rate = lax.axis_index("rate")
    row = lax.broadcasted_iota(jnp.int32, (total, total), 0)
    col = lax.broadcasted_iota(jnp.int32, (total, total), 1)
    part = (row // share) ^ rate
    source = (part * templ + row % templ) * 2 + row % share // templ
    choose = (col == source).astype(BF16)
    ordered = jnp.dot(choose, mixing[...], preferred_element_type=F32)
    live = lax.broadcasted_iota(jnp.int32, (total, basis), 1) < count[0]
    ordered = jnp.where(live, ordered, 0.0).astype(BF16)
    combined = jnp.dot(ordered, filters[...], preferred_element_type=F32)
    lags = filters.shape[1] // LANES
    low_half = lax.broadcasted_iota(jnp.int32, (total, LANES), 0) < share
    own, other = [], []
    for a in range(0, lags, 2):
        even = combined[:, a * LANES : (a + 1) * LANES]
        odd = combined[:, (a + 1) * LANES : (a + 2) * LANES]
        own.append(jnp.where(low_half, even, pltpu.roll(odd, share, 0)))
        other.append(jnp.where(low_half, pltpu.roll(even, share, 0), odd))
    out[...] = jnp.concatenate(own + other, axis=0).astype(BF16)


def band_kernel(series, upper_out, lower_out, lag_out):
    right = keep_right()
    for b in range(series.shape[0]):
        lag = jnp.zeros((1, 1), F32)
        for part in range(2):
            row = series[b, part : part + 1, :]
            fill = jnp.zeros((1, 3 * LANES - row.shape[1]), F32)
            row = jnp.concatenate([row, fill], axis=1)
            lag = lag + jnp.sum(row * row, axis=1, keepdims=True)
            before = jnp.zeros((LANES, LANES), F32)
            for d in range(3):
                now = circulant(row[:, d * LANES : (d + 1) * LANES])
                upper, lower = split_two(jnp.where(right, now, before))
                upper_out[b, part * LANES : (part + 1) * LANES, d * LANES : (d + 1) * LANES] = upper
                lower_out[b, part * LANES : (part + 1) * LANES, d * LANES : (d + 1) * LANES] = lower
                before = now
        lag_out[b] = jnp.broadcast_to(lag, (8, LANES))


def output_kernel(
    own_a, own_b, other_a, other_b, full, outer, band_up, band_low, lag,
    snr_out, chi_out, spec, logs, toeplitz, *, order, tms, length, taps, window,
):
    rows = length // LANES
    high = length // 2 // LANES
    spec_rows = 8 * high
    lags = taps // LANES
    lag_rows = lags * 4
    piece_rows = tms * spec_rows + 2 * lag_rows
    pieces = len(order) * tms
    behind = -(-(taps + window) // length)
    near = behind + 2
    banks = len(order)
    half = banks // 2
    bank = lax.axis_index("bank")
    tm = lax.axis_index("tm")
    place = bank * tms + tm
    bufs = ((own_a, own_b), (other_a, other_b))

    def piece(c, d):
        return bufs[c][d // half], (d % half) * piece_rows

    zero = jnp.zeros((4 * high, LANES), F32)
    for c in range(2):
        for i in range(behind):
            spec[c, i] = zero
            logs[c, i] = zero[:high]
        spec[c, pieces + behind] = zero
        logs[c, pieces + behind] = zero[:high]
        for d in range(banks):
            ref, start = piece(c, d)
            for e in range(tms):
                top = start + e * spec_rows
                value = ref[top : top + 4 * high].astype(F32)
                value = value + ref[top + 4 * high : top + 8 * high].astype(F32)
                spec[c, ((bank ^ order[d]) * tms + (tm ^ e)) + behind] = value

    def advance(g, states):
        nexts = []
        for c in range(2):
            drive = spec[c, g + behind, 2 * high : 3 * high]
            keep = spec[c, g + behind, 3 * high : 4 * high]
            nexts.append(keep * states[c] + drive)
            logs[c, g + behind] = nexts[c]
        return tuple(nexts)

    states = (zero[:high], zero[:high])
    if pieces <= 16:
        for g in range(pieces):
            states = advance(g, states)
    else:
        lax.fori_loop(0, pieces, advance, states)

    cos_one, sin_one = outer[0], outer[1]
    bin_row = lax.broadcasted_iota(jnp.int32, (high, LANES), 0)
    bin_lane = lax.broadcasted_iota(jnp.int32, (high, LANES), 1)
    weight = jnp.where(bin_row + bin_lane == 0, 1.0 / length, 2.0 / length).astype(F32)
    left = []
    for c in range(2):
        for i in range(near):
            scale = jnp.exp(-0.5 * logs[c, place + i]) * weight
            real = spec[c, place + i, :high] * scale
            imag = spec[c, place + i, high : 2 * high] * scale
            cos_parts, sin_parts = [], []
            for kh in range(high):
                re = jnp.broadcast_to(real[kh : kh + 1], (rows, LANES))
                im = jnp.broadcast_to(imag[kh : kh + 1], (rows, LANES))
                cos_parts.append(re * cos_one + im * sin_one)
                sin_parts.append(im * cos_one - re * sin_one)
            left.append(jnp.concatenate(cos_parts + sin_parts, axis=1))
    white = lax.dot_general(
        jnp.concatenate(left, axis=0),
        full[...],
        (((1,), (0,)), ((), ())),
        precision=HIGHEST,
        preferred_element_type=F32,
    )
    white = white.astype(BF16).astype(F32)

    first_out = behind * rows - 1
    out_frames = rows + 2
    first_t = first_out - (lags - 1)
    t_frames = lags - 1 + out_frames
    right = keep_right()
    for c in range(2):
        base = c * near * rows
        before = circulant(white[base + first_t - 1 : base + first_t])
        for s in range(t_frames):
            at = base + first_t + s
            now = circulant(white[at : at + 1])
            toeplitz[c * LANES : (c + 1) * LANES, s * LANES : (s + 1) * LANES] = jnp.where(
                right, now, before
            ).astype(BF16)
            before = now

    low_half = lax.broadcasted_iota(jnp.int32, (8, LANES), 0) < 4
    low_phase = lax.broadcasted_iota(jnp.int32, (8, LANES), 0) % 4 < 2
    after = jnp.where(place == pieces - 1, 0.0, 1.0).astype(F32)
    lane_row = lax.broadcasted_iota(jnp.int32, (LANES, LANES), 0)
    lane_col = lax.broadcasted_iota(jnp.int32, (LANES, LANES), 1)
    upto = (lane_row <= lane_col).astype(BF16)
    sums = jnp.concatenate([upto, jnp.ones((LANES, LANES), BF16)], axis=1)

    def conv(d):
        parts = []
        for c in range(2):
            ref, start = piece(c, d)
            top = start + tms * spec_rows + c * lag_rows
            parts.append(ref[top : top + lag_rows])
        return jnp.concatenate(parts, axis=1)

    def frames_of(g_all, row):
        accs = []
        for n in range(out_frames + 1):
            acc = None
            for a in range(lags // 2):
                s = n - 1 + (lags - 1) - 2 * a
                if 0 <= s < t_frames:
                    tile = g_all[row + 8 * a : row + 8 * a + 8, s * LANES : (s + 1) * LANES]
                    acc = tile if acc is None else acc + tile
            accs.append(acc)
        return [accs[n + 1] + pltpu.roll(accs[n], 4, 0) for n in range(out_frames)]

    for group in range(0, banks, 4):
        members = range(group, min(group + 4, banks))
        f_all = jnp.concatenate([conv(d) for d in members], axis=0)
        g_all = jnp.dot(f_all, toeplitz[...], preferred_element_type=F32)
        for first in range(0, len(members), 2):
            d0, d1 = members[first], members[first + 1]
            bank0, bank1 = bank ^ order[d0], bank ^ order[d1]
            z0 = frames_of(g_all, first * lag_rows)
            z1 = frames_of(g_all, (first + 1) * lag_rows)
            z = [jnp.where(low_half, p, pltpu.roll(q, 4, 0)) for p, q in zip(z0, z1)]
            z[-1] = z[-1] * after
            stacked = jnp.concatenate(
                [jnp.concatenate(z[n : n + rows], axis=0) for n in range(3)], axis=1
            )
            up, low = split_two(stacked)
            corr = []
            for d in (d0, d1):
                b_up = band_up[bank ^ order[d]]
                b_low = band_low[bank ^ order[d]]
                dims = (((1,), (1,)), ((), ()))
                corr.append(
                    lax.dot_general(up, b_up, dims, preferred_element_type=F32)
                    + lax.dot_general(low, b_up, dims, preferred_element_type=F32)
                    + lax.dot_general(up, b_low, dims, preferred_element_type=F32)
                )
            power = []
            for v in z:
                square = v * v
                power.append(square + pltpu.roll(square, 6, 0))
            p_up, p_low = split_two(jnp.concatenate(power, axis=0))
            run = jnp.dot(p_up, sums, preferred_element_type=F32) + jnp.dot(
                p_low, sums, preferred_element_type=F32
            )
            lag_now = jnp.where(low_half, lag[bank0], lag[bank1])
            for n in range(rows):
                tile = slice(8 * n, 8 * n + 8)
                c_re = jnp.where(low_half, corr[0][tile, :LANES], corr[1][tile, :LANES])
                c_im = jnp.where(low_half, corr[0][tile, LANES:], corr[1][tile, LANES:])
                mid = z[n + 1]
                turned = jnp.where(low_phase, -pltpu.roll(mid, 6, 0), pltpu.roll(mid, 2, 0))
                cross = mid * c_re + turned * c_im
                cross = cross + pltpu.roll(cross, 6, 0)
                prev = slice(8 * n, 8 * n + 8)
                here = slice(8 * n + 8, 8 * n + 16)
                nxt = slice(8 * n + 16, 8 * n + 24)
                win = (run[prev, LANES:] - run[prev, :LANES] + power[n]) + (
                    run[here, LANES:] + run[nxt, :LANES]
                )
                energy = power[n + 1]
                chi = (win - 2.0 * cross + energy * lag_now) / (2 * window + 1)
                lanes = slice(n * LANES, (n + 1) * LANES)
                snr_out[bank0, :, lanes] = energy[0:2]
                snr_out[bank1, :, lanes] = energy[4:6]
                chi_out[bank0, :, lanes] = chi[0:2]
                chi_out[bank1, :, lanes] = chi[4:6]


ON_CHIP_BYTES = 3 * 2**20


def on_chip(*arrays):
    if sum(a.size * a.dtype.itemsize for a in arrays) > ON_CHIP_BYTES:
        return arrays
    return [pltpu.with_memory_space_constraint(a, pltpu.VMEM) for a in arrays]


def on_chip_shape(shape, dtype):
    if 2 * math.prod(shape) * jnp.dtype(dtype).itemsize > ON_CHIP_BYTES:
        return jax.ShapeDtypeStruct(shape, dtype)
    return pltpu.VMEM(shape, dtype)


VMEM = pl.BlockSpec(memory_space=pltpu.VMEM)
SMEM = pl.BlockSpec(memory_space=pltpu.SMEM)


def body(
    strain, gate_mask, psd_reset, psd_ref, psd_rate, filters, basis_count, mixing, autocorrelation
):
    length = strain.shape[1]
    rows = length // LANES
    high = length // 2 // LANES
    banks = lax.axis_size("bank")
    tms = lax.axis_size("tm")
    basis, taps = filters.shape[2:]
    templ = mixing.shape[2]
    window = autocorrelation.shape[2] // 2
    lags = taps // LANES
    outer, inner, shift, full = tables(length)

    spec = pl.pallas_call(
        spectrum_kernel,
        out_shape=pltpu.VMEM((8 * high, LANES), BF16),
        in_specs=[VMEM, VMEM, SMEM] + [VMEM] * 5,
        out_specs=VMEM,
        name="spectrum",
    )(
        strain.reshape(rows, LANES),
        gate_mask.reshape(rows, LANES),
        psd_reset,
        psd_ref.reshape(high, LANES),
        psd_rate.reshape(high, LANES),
        outer,
        inner,
        shift,
    )
    combined = pl.pallas_call(
        filter_kernel,
        out_shape=pltpu.VMEM((2 * templ * lags, LANES), BF16),
        in_specs=[VMEM, VMEM, SMEM],
        out_specs=VMEM,
        name="filters",
    )(filters.reshape(basis, taps), mixing.reshape(2 * templ, basis), basis_count)
    band = on_chip_shape((banks, 2 * LANES, 3 * LANES), BF16)
    band_up, band_low, lag = pl.pallas_call(
        band_kernel,
        out_shape=(band, band, pltpu.VMEM((banks, 8, LANES), F32)),
        in_specs=[VMEM],
        out_specs=(VMEM, VMEM, VMEM),
        name="bands",
    )(autocorrelation)

    distance = 1
    while distance < tms:
        spec = jnp.concatenate([spec, swapped(spec, "tm", distance)])
        distance *= 2
    held = jnp.concatenate([spec, combined])
    distance = banks // 2
    order = [0]
    while distance > 1:
        held = jnp.concatenate([held, swapped(held, "bank", distance)])
        order = order + [d ^ distance for d in order]
        distance //= 2
    far = swapped(held, "bank", 1)
    order = order + [d ^ 1 for d in order]
    held_other = swapped(held, "rate", 1)
    far_other = swapped(far, "rate", 1)

    behind = -(-(taps + window) // length)
    share = templ // 2
    out = jax.ShapeDtypeStruct((banks, share, length), F32)
    return pl.pallas_call(
        functools.partial(
            output_kernel, order=tuple(order), tms=tms, length=length, taps=taps, window=window
        ),
        out_shape=(out, out),
        in_specs=[VMEM] * 9,
        out_specs=(VMEM, VMEM),
        scratch_shapes=[
            pltpu.VMEM((2, banks * tms + behind + 1, 4 * high, LANES), F32),
            pltpu.VMEM((2, banks * tms + behind + 1, high, LANES), F32),
            pltpu.VMEM((2 * LANES, (lags + rows + 1) * LANES), BF16),
        ],
        name="outputs",
    )(*on_chip(held, far, held_other, far_other, full, outer, band_up, band_low, lag))


def solution(mesh):
    return jax.shard_map(
        body,
        mesh=mesh,
        in_specs=(
            P("rate", ("parts", "bank", "tm")),
            P(("parts", "bank", "tm")),
            P(("parts", "bank", "tm")),
            P("rate", None),
            P("rate", None),
            P("bank", "rate", None, None),
            P("bank"),
            P("bank", "rate", None, None, None),
            P(),
        ),
        out_specs=(
            P(None, "rate", ("parts", "bank", "tm")),
            P(None, "rate", ("parts", "bank", "tm")),
        ),
        check_vma=False,
    )
```

```python
import functools
import math

import jax
import jax.numpy as jnp
import numpy as np
from jax import lax
from jax.experimental import pallas as pl
from jax.experimental.pallas import tpu as pltpu
from jax.sharding import PartitionSpec as P


LANES = 128
F32 = jnp.float32
BF16 = jnp.bfloat16


def swapped(block, axis, distance):
    route = [(i, i ^ distance) for i in range(lax.axis_size(axis))]
    return lax.ppermute(block, axis, route)


def two_terms(table):
    upper = table.astype(BF16)
    return upper, (table - upper.astype(np.float32)).astype(BF16)


def tables(length):
    rows = length // LANES
    high = length // 2 // LANES
    lane = np.arange(LANES)
    turn = 2.0 * math.pi
    outer = turn * (np.arange(rows)[:, None] * lane[None, :] % rows) / rows
    outer = np.stack([np.cos(outer), np.sin(outer)])
    shift = turn * (np.arange(high)[:, None] * lane[None, :] % rows) / rows
    shift = np.stack([np.cos(shift), np.sin(shift)])
    step = 8
    fine = turn * (np.arange(step)[:, None] * lane[None, :]) / length
    coarse = turn * (np.arange(0, LANES, step)[:, None] * lane[None, :]) / length
    start = np.concatenate([np.cos(fine), np.sin(fine), np.cos(coarse), np.sin(coarse)])
    bins = np.arange(length // 2)
    full = turn * (bins[:, None] * lane[None, :] % length) / length
    full = np.concatenate([np.cos(full), np.sin(full)], axis=0)
    outer, shift, start, full = (a.astype(np.float32) for a in (outer, shift, start, full))
    return outer, shift, start, np.concatenate(two_terms(full), axis=1)


def split_two(value):
    upper = value.astype(BF16)
    return upper, (value - upper.astype(F32)).astype(BF16)


def product_two(left, right):
    upper, lower = split_two(left)
    count, width = left.shape[0], right.shape[1] // 2
    both = jnp.dot(jnp.concatenate([upper, lower], axis=0), right, preferred_element_type=F32)
    small = (both[:count, width:] + both[count:, width:]) + both[count:, :width]
    return both[:count, :width] + small


def circulant(row):
    return pltpu.roll(jnp.broadcast_to(row, (LANES, LANES)), 0, 1, stride=1, stride_axis=0)


def keep_right():
    u = lax.broadcasted_iota(jnp.int32, (LANES, LANES), 0)
    q = lax.broadcasted_iota(jnp.int32, (LANES, LANES), 1)
    return q >= u


def spectrum_kernel(strain, mask, reset, psd_ref, psd_rate, outer, shift, start, out):
    rows = strain.shape[0]
    high = psd_ref.shape[0]
    signal = strain[...] * mask[...].astype(F32)
    reference_psd = psd_ref[...]
    rate = psd_rate[...]
    step = start.shape[0] // 2 - LANES // 8
    fine_c, fine_s = start[:step], start[step : 2 * step]
    wide_c, wide_s = start[2 * step : 2 * step + LANES // 8], start[2 * step + LANES // 8 :]
    cos_rows, sin_rows = [], []
    for a in range(LANES // 8):
        c, s = wide_c[a : a + 1], wide_s[a : a + 1]
        cos_rows.append(c * fine_c - s * fine_s)
        sin_rows.append(s * fine_c + c * fine_s)
    cos_all, sin_all = jnp.concatenate(cos_rows, axis=0), jnp.concatenate(sin_rows, axis=0)
    terms = [split_two(v) for v in (cos_all, sin_all)]
    inner = jnp.concatenate([terms[0][0], terms[1][0], terms[0][1], terms[1][1]], axis=1)
    left = [signal * shift[i, k : k + 1] for i in range(2) for k in range(high)]
    product = product_two(jnp.concatenate(left, axis=0), inner)
    cos_one, sin_one = outer[0], outer[1]
    real_rows, imag_rows = [], []
    for kh in range(high):
        with_cos = product[kh * rows : (kh + 1) * rows]
        with_sin = product[(high + kh) * rows : (high + kh + 1) * rows]
        cos_sum = with_cos[:, :LANES] - with_sin[:, LANES:]
        sin_sum = with_cos[:, LANES:] + with_sin[:, :LANES]
        real_rows.append(jnp.sum(cos_one * cos_sum - sin_one * sin_sum, axis=0, keepdims=True))
        imag_rows.append(jnp.sum(sin_one * cos_sum + cos_one * sin_sum, axis=0, keepdims=True))
    real_part = jnp.concatenate(real_rows, axis=0)
    imag_part = jnp.concatenate(imag_rows, axis=0)
    power = (real_part * real_part + imag_part * imag_part) / (rows * LANES / 2)
    log_power = jnp.log(power + 0.1 * reference_psd)
    keep = (1.0 - rate) * (1.0 - 0.5 * reset[0].astype(F32))
    first = (lax.axis_index("bank") == 0) & (lax.axis_index("tm") == 0)
    drive = rate * log_power + jnp.where(first, keep * jnp.log(reference_psd), 0.0)
    whole = jnp.concatenate([real_part, imag_part, drive, keep], axis=0)
    upper, lower = split_two(whole)
    out[: 4 * high] = upper
    out[4 * high :] = lower


def filter_kernel(filters, mixing, count, out):
    total, basis = mixing.shape
    share = total // 2
    templ = share // 2
    rate = lax.axis_index("rate")
    row = lax.broadcasted_iota(jnp.int32, (total, total), 0)
    col = lax.broadcasted_iota(jnp.int32, (total, total), 1)
    part = (row // share) ^ rate
    source = (part * templ + row % templ) * 2 + row % share // templ
    choose = (col == source).astype(BF16)
    ordered = jnp.dot(choose, mixing[...], preferred_element_type=F32)
    live = lax.broadcasted_iota(jnp.int32, (total, basis), 1) < count[0]
    ordered = jnp.where(live, ordered, 0.0).astype(BF16)
    combined = jnp.dot(ordered, filters[...], preferred_element_type=F32)
    lags = filters.shape[1] // LANES
    low_half = lax.broadcasted_iota(jnp.int32, (total, LANES), 0) < share
    own, other = [], []
    for a in range(0, lags, 2):
        even = combined[:, a * LANES : (a + 1) * LANES]
        odd = combined[:, (a + 1) * LANES : (a + 2) * LANES]
        own.append(jnp.where(low_half, even, pltpu.roll(odd, share, 0)))
        other.append(jnp.where(low_half, pltpu.roll(even, share, 0), odd))
    out[...] = jnp.concatenate(own + other, axis=0).astype(BF16)


def band_kernel(series, upper_out, lower_out, lag_out):
    right = keep_right()
    for b in range(series.shape[0]):
        lag = jnp.zeros((1, 1), F32)
        for part in range(2):
            row = series[b, part : part + 1, :]
            lag = lag + jnp.sum(row * row, axis=1, keepdims=True)
            fill = jnp.zeros((1, 3 * LANES - row.shape[1]), F32)
            row = jnp.concatenate([row, fill], axis=1)
            before = jnp.zeros((LANES, LANES), F32)
            for d in range(3):
                now = circulant(row[:, d * LANES : (d + 1) * LANES])
                upper, lower = split_two(jnp.where(right, now, before))
                upper_out[b, d, part * LANES : (part + 1) * LANES] = upper
                lower_out[b, d, part * LANES : (part + 1) * LANES] = lower
                before = now
        lag_out[b] = jnp.broadcast_to(lag, (8, LANES))


def output_kernel(
    own_a, own_b, other_a, other_b, full, outer, band_up, band_low, lag,
    snr_out, chi_out, spec, logs, *, order, tms, length, taps, window,
):
    rows = length // LANES
    high = length // 2 // LANES
    spec_rows = 8 * high
    lags = taps // LANES
    lag_rows = lags * 4
    piece_rows = tms * spec_rows + 2 * lag_rows
    pieces = len(order) * tms
    behind = -(-(taps + window) // length)
    near = behind + 2
    banks = len(order)
    half = banks // 2
    bank = lax.axis_index("bank")
    tm = lax.axis_index("tm")
    place = bank * tms + tm
    bufs = ((own_a, own_b), (other_a, other_b))

    def piece(c, d):
        return bufs[c][d // half], (d % half) * piece_rows

    zero = jnp.zeros((4 * high, LANES), F32)
    for c in range(2):
        for i in range(behind):
            spec[c, i] = zero
            logs[c, i] = zero[:high]
        spec[c, pieces + behind] = zero
        logs[c, pieces + behind] = zero[:high]
        for d in range(banks):
            ref, start = piece(c, d)
            for e in range(tms):
                top = start + e * spec_rows
                value = ref[top : top + 4 * high].astype(F32)
                value = value + ref[top + 4 * high : top + 8 * high].astype(F32)
                spec[c, ((bank ^ order[d]) * tms + (tm ^ e)) + behind] = value

    def advance(g, states):
        nexts = []
        for c in range(2):
            drive = spec[c, g + behind, 2 * high : 3 * high]
            keep = spec[c, g + behind, 3 * high : 4 * high]
            nexts.append(keep * states[c] + drive)
            logs[c, g + behind] = nexts[c]
        return tuple(nexts)

    states = (zero[:high], zero[:high])
    if pieces <= 16:
        for g in range(pieces):
            states = advance(g, states)
    else:
        lax.fori_loop(0, pieces, advance, states)

    cos_one, sin_one = outer[0], outer[1]
    bin_row = lax.broadcasted_iota(jnp.int32, (high, LANES), 0)
    bin_lane = lax.broadcasted_iota(jnp.int32, (high, LANES), 1)
    weight = jnp.where(bin_row + bin_lane == 0, 1.0 / length, 2.0 / length).astype(F32)
    top_row = lax.broadcasted_iota(jnp.int32, (rows, LANES), 0) == 0
    left = []
    for c in range(2):
        real, imag = [], []
        for i in range(near):
            scale = jnp.exp(-0.5 * logs[c, place + i]) * weight
            real.append(spec[c, place + i, :high] * scale)
            imag.append(spec[c, place + i, high : 2 * high] * scale)
        for i in range(near - 1):
            cos_parts, sin_parts = [], []
            for kh in range(high):
                re = jnp.broadcast_to(real[i][kh : kh + 1], (rows, LANES))
                im = jnp.broadcast_to(imag[i][kh : kh + 1], (rows, LANES))
                if i == 0:
                    re = jnp.where(top_row, real[near - 1][kh : kh + 1], re)
                    im = jnp.where(top_row, imag[near - 1][kh : kh + 1], im)
                cos_parts.append(re * cos_one + im * sin_one)
                sin_parts.append(im * cos_one - re * sin_one)
            left.append(jnp.concatenate(cos_parts + sin_parts, axis=1))
    white = product_two(jnp.concatenate(left, axis=0), full[...])
    white = white.astype(BF16).astype(F32)

    first_out = behind * rows - 1
    out_frames = rows + 2
    first_t = first_out - (lags - 1)
    t_frames = lags - 1 + out_frames
    assert first_t == rows and first_t + t_frames - 1 == (near - 1) * rows
    right = keep_right()

    def frame(c, s):
        at = c * (near - 1) * rows + (first_t + s) % ((near - 1) * rows)
        return circulant(white[at : at + 1])

    earlier = [
        circulant(white[top : top + 1])
        for top in (first_t - 1, (near - 1) * rows + first_t - 1)
    ]
    toeplitz = []
    for s in range(t_frames):
        tiles = []
        for c in range(2):
            now = frame(c, s)
            tiles.append(jnp.where(right, now, earlier[c]).astype(BF16))
            earlier[c] = now
        toeplitz.append(jnp.concatenate(tiles, axis=0))

    low_half = lax.broadcasted_iota(jnp.int32, (8, LANES), 0) < 4
    low_phase = lax.broadcasted_iota(jnp.int32, (8, LANES), 0) % 4 < 2
    after = jnp.where(place == pieces - 1, 0.0, 1.0).astype(F32)
    lane_row = lax.broadcasted_iota(jnp.int32, (LANES, LANES), 0)
    lane_col = lax.broadcasted_iota(jnp.int32, (LANES, LANES), 1)
    upto = (lane_row <= lane_col).astype(BF16)
    sums = jnp.concatenate([upto, jnp.ones((LANES, LANES), BF16)], axis=1)

    def conv(d):
        parts = []
        for c in range(2):
            ref, start = piece(c, d)
            top = start + tms * spec_rows + c * lag_rows
            parts.append(ref[top : top + lag_rows])
        return jnp.concatenate(parts, axis=1)

    def convolved(members):
        count = len(members)
        filt = [conv(d) for d in members]
        f_all = jnp.concatenate(
            [f[top : top + 16] for top in range(0, lag_rows, 16) for f in filt], axis=0
        )
        accs = [[None] * (out_frames + 1) for _ in members]
        for s in range(0, t_frames, 2):
            both = range(s, min(s + 2, t_frames))
            valid = [
                (a, t, t - (lags - 2) + 2 * a)
                for a in range(lags // 2)
                for t in both
                if 0 <= t - (lags - 2) + 2 * a <= out_frames
            ]
            low = min(a for a, _, _ in valid) // 2
            top = max(a for a, _, _ in valid) // 2 + 1
            g = jnp.dot(
                f_all[low * 16 * count : top * 16 * count],
                jnp.concatenate([toeplitz[t] for t in both], axis=1),
                preferred_element_type=F32,
            )
            for a, t, n in valid:
                for k in range(count):
                    row = ((a // 2 - low) * count + k) * 16 + a % 2 * 8
                    tile = g[row : row + 8, (t - s) * LANES : (t - s + 1) * LANES]
                    accs[k][n] = tile if accs[k][n] is None else accs[k][n] + tile
        return [
            [acc[n + 1] + pltpu.roll(acc[n], 4, 0) for n in range(out_frames)] for acc in accs
        ]

    def outputs(pair, z, corr, power, run):
        lag_now = jnp.where(low_half, lag[pair[0]], lag[pair[1]])
        for n in range(rows):
            tile = slice(8 * n, 8 * n + 8)
            c_re = jnp.where(low_half, corr[0][tile, :LANES], corr[1][tile, :LANES])
            c_im = jnp.where(low_half, corr[0][tile, LANES:], corr[1][tile, LANES:])
            mid = z[n + 1]
            turned = jnp.where(low_phase, -pltpu.roll(mid, 6, 0), pltpu.roll(mid, 2, 0))
            cross = mid * c_re + turned * c_im
            cross = cross + pltpu.roll(cross, 6, 0)
            here = slice(8 * n + 8, 8 * n + 16)
            after_it = slice(8 * n + 16, 8 * n + 24)
            win = (run[tile, LANES:] - run[tile, :LANES] + power[n]) + (
                run[here, LANES:] + run[after_it, :LANES]
            )
            energy = power[n + 1]
            chi = (win - 2.0 * cross + energy * lag_now) / (2 * window + 1)
            lanes = slice(n * LANES, (n + 1) * LANES)
            for top, member in zip((0, 4), pair):
                snr_out[member, :, lanes] = energy[top : top + 2]
                chi_out[member, :, lanes] = chi[top : top + 2]

    dims = (((1,), (1,)), ((), ()))
    for group in range(0, banks, 4):
        members = range(group, min(group + 4, banks))
        frames = convolved(members)
        z_all, power_all, pairs, corr_all = [], [], [], []
        for first in range(0, len(members), 2):
            pairs.append([bank ^ order[d] for d in members[first : first + 2]])
            z0, z1 = frames[first], frames[first + 1]
            z = [jnp.where(low_half, p, pltpu.roll(q, 4, 0)) for p, q in zip(z0, z1)]
            z[-1] = z[-1] * after
            z_all.append(z)
        for z, pair in zip(z_all, pairs):
            stacked = jnp.concatenate(
                [jnp.concatenate(z[n : n + rows], axis=0) for n in range(3)], axis=1
            )
            up, low = split_two(stacked)
            both = jnp.concatenate([up, low], axis=0)
            count = up.shape[0]
            corr = []
            for member in pair:
                b_up = jnp.concatenate([band_up[member, d] for d in range(3)], axis=1)
                b_low = jnp.concatenate([band_low[member, d] for d in range(3)], axis=1)
                one = lax.dot_general(both, b_up, dims, preferred_element_type=F32)
                two = lax.dot_general(up, b_low, dims, preferred_element_type=F32)
                corr.append(one[:count] + one[count:] + two)
            corr_all.append(corr)
            squares = [v * v for v in z]
            power_all.append([v + pltpu.roll(v, 6, 0) for v in squares])
        stacked = jnp.concatenate([v for power in power_all for v in power], axis=0)
        up, low = split_two(stacked)
        run_all = jnp.dot(
            jnp.concatenate([up, low], axis=0), sums, preferred_element_type=F32
        )
        count = stacked.shape[0]
        run_all = run_all[:count] + run_all[count:]
        step = 8 * out_frames
        for k, pair in enumerate(pairs):
            run = run_all[k * step : (k + 1) * step]
            outputs(pair, z_all[k], corr_all[k], power_all[k], run)


ON_CHIP_BYTES = 3 * 2**20


def on_chip(*arrays):
    if sum(a.size * a.dtype.itemsize for a in arrays) > ON_CHIP_BYTES:
        return arrays
    return [pltpu.with_memory_space_constraint(a, pltpu.VMEM) for a in map(jnp.asarray, arrays)]


def on_chip_shape(shape, dtype):
    if 2 * math.prod(shape) * jnp.dtype(dtype).itemsize > ON_CHIP_BYTES:
        return jax.ShapeDtypeStruct(shape, dtype)
    return pltpu.VMEM(shape, dtype)


VMEM = pl.BlockSpec(memory_space=pltpu.VMEM)
SMEM = pl.BlockSpec(memory_space=pltpu.SMEM)


def body(
    strain, gate_mask, psd_reset, psd_ref, psd_rate, filters, basis_count, mixing, autocorrelation
):
    length = strain.shape[1]
    rows = length // LANES
    high = length // 2 // LANES
    banks = lax.axis_size("bank")
    tms = lax.axis_size("tm")
    basis, taps = filters.shape[2:]
    templ = mixing.shape[2]
    window = autocorrelation.shape[2] // 2
    lags = taps // LANES
    outer, shift, start, full = tables(length)

    spec = pl.pallas_call(
        spectrum_kernel,
        out_shape=pltpu.VMEM((8 * high, LANES), BF16),
        in_specs=[VMEM, VMEM, SMEM] + [VMEM] * 5,
        out_specs=VMEM,
        name="spectrum",
    )(
        strain.reshape(rows, LANES),
        gate_mask.reshape(rows, LANES),
        psd_reset,
        psd_ref.reshape(high, LANES),
        psd_rate.reshape(high, LANES),
        outer,
        shift,
        start,
    )
    combined = pl.pallas_call(
        filter_kernel,
        out_shape=pltpu.VMEM((2 * templ * lags, LANES), BF16),
        in_specs=[VMEM, VMEM, SMEM],
        out_specs=VMEM,
        name="filters",
    )(filters.reshape(basis, taps), mixing.reshape(2 * templ, basis), basis_count)
    band = on_chip_shape((banks, 3, 2 * LANES, LANES), BF16)
    band_up, band_low, lag = pl.pallas_call(
        band_kernel,
        out_shape=(band, band, pltpu.VMEM((banks, 8, LANES), F32)),
        in_specs=[VMEM],
        out_specs=(VMEM, VMEM, VMEM),
        name="bands",
    )(autocorrelation)

    distance = 1
    while distance < tms:
        spec = jnp.concatenate([spec, swapped(spec, "tm", distance)])
        distance *= 2
    held = jnp.concatenate([spec, combined])
    distance = banks // 2
    order = [0]
    while distance > 1:
        held = jnp.concatenate([held, swapped(held, "bank", distance)])
        order = order + [d ^ distance for d in order]
        distance //= 2
    far = swapped(held, "bank", 1)
    order = order + [d ^ 1 for d in order]
    held_other = swapped(held, "rate", 1)
    far_other = swapped(far, "rate", 1)

    behind = -(-(taps + window) // length)
    share = templ // 2
    out = jax.ShapeDtypeStruct((banks, share, length), F32)
    return pl.pallas_call(
        functools.partial(
            output_kernel, order=tuple(order), tms=tms, length=length, taps=taps, window=window
        ),
        out_shape=(out, out),
        in_specs=[VMEM] * 9,
        out_specs=(VMEM, VMEM),
        scratch_shapes=[
            pltpu.VMEM((2, banks * tms + behind + 1, 4 * high, LANES), F32),
            pltpu.VMEM((2, banks * tms + behind + 1, high, LANES), F32),
        ],
        name="outputs",
    )(*on_chip(held, far, held_other, far_other, full, outer, band_up, band_low, lag))


def solution(mesh):
    return jax.shard_map(
        body,
        mesh=mesh,
        in_specs=(
            P("rate", ("parts", "bank", "tm")),
            P(("parts", "bank", "tm")),
            P(("parts", "bank", "tm")),
            P("rate", None),
            P("rate", None),
            P("bank", "rate", None, None),
            P("bank"),
            P("bank", "rate", None, None, None),
            P(),
        ),
        out_specs=(
            P(None, "rate", ("parts", "bank", "tm")),
            P(None, "rate", ("parts", "bank", "tm")),
        ),
        check_vma=False,
    )
```

```python
import functools
import math

import jax
import jax.numpy as jnp
import numpy as np
from jax import lax
from jax.experimental import pallas as pl
from jax.experimental.pallas import tpu as pltpu
from jax.sharding import PartitionSpec as P


LANES = 128
F32 = jnp.float32
BF16 = jnp.bfloat16


def swapped(block, axis, distance):
    count = lax.axis_size("rate")
    places = range(lax.axis_size(axis) * count)
    route = [(i, (i // count ^ distance) * count + (i % count ^ 1)) for i in places]
    return lax.ppermute(block, (axis, "rate"), route)


def swapped_cores(block):
    return lax.ppermute(block, "rate", [(i, i ^ 1) for i in range(lax.axis_size("rate"))])


def two_terms(table):
    upper = table.astype(BF16)
    return upper, (table - upper.astype(np.float32)).astype(BF16)


def tables(length):
    rows = length // LANES
    high = length // 2 // LANES
    lane = np.arange(LANES)
    turn = 2.0 * math.pi
    outer = turn * (np.arange(rows)[:, None] * lane[None, :] % rows) / rows
    outer = np.stack([np.cos(outer), np.sin(outer)])
    shift = turn * (np.arange(high)[:, None] * lane[None, :] % rows) / rows
    shift = np.stack([np.cos(shift), np.sin(shift)])
    step = 8
    fine = turn * (np.arange(step)[:, None] * lane[None, :]) / length
    coarse = turn * (np.arange(0, LANES, step)[:, None] * lane[None, :]) / length
    start = np.concatenate([np.cos(fine), np.sin(fine), np.cos(coarse), np.sin(coarse)])
    bins = np.arange(length // 2)
    full = turn * (bins[:, None] * lane[None, :] % length) / length
    full = np.concatenate([np.cos(full), np.sin(full)], axis=0)
    outer, shift, start, full = (a.astype(np.float32) for a in (outer, shift, start, full))
    return outer, shift, start, np.concatenate(two_terms(full), axis=1)


def split_two(value):
    upper = value.astype(BF16)
    return upper, (value - upper.astype(F32)).astype(BF16)


def product_two(left, right):
    upper, lower = split_two(left)
    count, width = left.shape[0], right.shape[1] // 2
    both = jnp.dot(jnp.concatenate([upper, lower], axis=0), right, preferred_element_type=F32)
    small = (both[:count, width:] + both[count:, width:]) + both[count:, :width]
    return both[:count, :width] + small


def circulant(row):
    return pltpu.roll(jnp.broadcast_to(row, (LANES, LANES)), 0, 1, stride=1, stride_axis=0)


def keep_right():
    u = lax.broadcasted_iota(jnp.int32, (LANES, LANES), 0)
    q = lax.broadcasted_iota(jnp.int32, (LANES, LANES), 1)
    return q >= u


def spectrum_kernel(strain, mask, reset, psd_ref, psd_rate, outer, shift, start, out):
    rows = strain.shape[0]
    high = psd_ref.shape[0]
    signal = strain[...] * mask[...].astype(F32)
    reference_psd = psd_ref[...]
    rate = psd_rate[...]
    step = start.shape[0] // 2 - LANES // 8
    fine_c, fine_s = start[:step], start[step : 2 * step]
    wide_c, wide_s = start[2 * step : 2 * step + LANES // 8], start[2 * step + LANES // 8 :]
    cos_rows, sin_rows = [], []
    for a in range(LANES // 8):
        c, s = wide_c[a : a + 1], wide_s[a : a + 1]
        cos_rows.append(c * fine_c - s * fine_s)
        sin_rows.append(s * fine_c + c * fine_s)
    cos_all, sin_all = jnp.concatenate(cos_rows, axis=0), jnp.concatenate(sin_rows, axis=0)
    terms = [split_two(v) for v in (cos_all, sin_all)]
    inner = jnp.concatenate([terms[0][0], terms[1][0], terms[0][1], terms[1][1]], axis=1)
    left = [signal * shift[i, k : k + 1] for i in range(2) for k in range(high)]
    product = product_two(jnp.concatenate(left, axis=0), inner)
    cos_one, sin_one = outer[0], outer[1]
    real_rows, imag_rows = [], []
    for kh in range(high):
        with_cos = product[kh * rows : (kh + 1) * rows]
        with_sin = product[(high + kh) * rows : (high + kh + 1) * rows]
        cos_sum = with_cos[:, :LANES] - with_sin[:, LANES:]
        sin_sum = with_cos[:, LANES:] + with_sin[:, :LANES]
        real_rows.append(jnp.sum(cos_one * cos_sum - sin_one * sin_sum, axis=0, keepdims=True))
        imag_rows.append(jnp.sum(sin_one * cos_sum + cos_one * sin_sum, axis=0, keepdims=True))
    real_part = jnp.concatenate(real_rows, axis=0)
    imag_part = jnp.concatenate(imag_rows, axis=0)
    power = (real_part * real_part + imag_part * imag_part) / (rows * LANES / 2)
    log_power = jnp.log(power + 0.1 * reference_psd)
    keep = (1.0 - rate) * (1.0 - 0.5 * reset[0].astype(F32))
    first = (lax.axis_index("bank") == 0) & (lax.axis_index("tm") == 0)
    drive = rate * log_power + jnp.where(first, keep * jnp.log(reference_psd), 0.0)
    whole = jnp.concatenate([real_part, imag_part, drive, keep], axis=0)
    upper, lower = split_two(whole)
    out[: 4 * high] = upper
    out[4 * high :] = lower


def filter_kernel(filters, mixing, count, out):
    total, basis = mixing.shape
    share = total // 2
    templ = share // 2
    rate = lax.axis_index("rate")
    row = lax.broadcasted_iota(jnp.int32, (total, total), 0)
    col = lax.broadcasted_iota(jnp.int32, (total, total), 1)
    part = (row // share) ^ rate
    source = (part * templ + row % templ) * 2 + row % share // templ
    choose = (col == source).astype(BF16)
    ordered = jnp.dot(choose, mixing[...], preferred_element_type=F32)
    live = lax.broadcasted_iota(jnp.int32, (total, basis), 1) < count[0]
    ordered = jnp.where(live, ordered, 0.0).astype(BF16)
    combined = jnp.dot(ordered, filters[...], preferred_element_type=F32)
    lags = filters.shape[1] // LANES
    low_half = lax.broadcasted_iota(jnp.int32, (total, LANES), 0) < share
    own, other = [], []
    for a in range(0, lags, 2):
        even = combined[:, a * LANES : (a + 1) * LANES]
        odd = combined[:, (a + 1) * LANES : (a + 2) * LANES]
        own.append(jnp.where(low_half, even, pltpu.roll(odd, share, 0)))
        other.append(jnp.where(low_half, pltpu.roll(even, share, 0), odd))
    out[...] = jnp.concatenate(own + other, axis=0).astype(BF16)


def band_kernel(series, upper_out, lower_out, lag_out):
    right = keep_right()
    for b in range(series.shape[0]):
        lag = jnp.zeros((1, 1), F32)
        for part in range(2):
            row = series[b, part : part + 1, :]
            lag = lag + jnp.sum(row * row, axis=1, keepdims=True)
            fill = jnp.zeros((1, 3 * LANES - row.shape[1]), F32)
            row = jnp.concatenate([row, fill], axis=1)
            before = jnp.zeros((LANES, LANES), F32)
            for d in range(3):
                now = circulant(row[:, d * LANES : (d + 1) * LANES])
                upper, lower = split_two(jnp.where(right, now, before))
                upper_out[b, d, part * LANES : (part + 1) * LANES] = upper
                lower_out[b, d, part * LANES : (part + 1) * LANES] = lower
                before = now
        lag_out[b] = jnp.broadcast_to(lag, (8, LANES))


def output_kernel(
    own_a, own_b, other_a, other_b, full, outer, band_up, band_low, lag,
    snr_out, chi_out, spec, logs, *, slots, tms, length, taps, window,
):
    rows = length // LANES
    high = length // 2 // LANES
    spec_rows = 8 * high
    lags = taps // LANES
    lag_rows = lags * 4
    piece_rows = tms * spec_rows + 2 * lag_rows
    pieces = len(slots) * tms
    behind = -(-(taps + window) // length)
    near = behind + 2
    banks = len(slots)
    half = banks // 2
    bank = lax.axis_index("bank")
    tm = lax.axis_index("tm")
    place = bank * tms + tm
    bufs = ((own_a, own_b), (other_a, other_b))

    def piece(c, d):
        return bufs[c][d // half], (d % half) * piece_rows

    zero = jnp.zeros((4 * high, LANES), F32)
    for c in range(2):
        for i in range(behind):
            spec[c, i] = zero
            logs[c, i] = zero[:high]
        spec[c, pieces + behind] = zero
        logs[c, pieces + behind] = zero[:high]
        for k, (d, crossed) in enumerate(slots):
            ref, start = piece(c, k)
            for e in range(tms):
                top = start + e * spec_rows
                value = ref[top : top + 4 * high].astype(F32)
                value = value + ref[top + 4 * high : top + 8 * high].astype(F32)
                band = c ^ crossed ^ (e.bit_count() & 1)
                spec[band, (bank ^ d) * tms + (tm ^ e) + behind] = value

    def advance(g, states):
        nexts = []
        for c in range(2):
            drive = spec[c, g + behind, 2 * high : 3 * high]
            keep = spec[c, g + behind, 3 * high : 4 * high]
            nexts.append(keep * states[c] + drive)
            logs[c, g + behind] = nexts[c]
        return tuple(nexts)

    states = (zero[:high], zero[:high])
    if pieces <= 16:
        for g in range(pieces):
            states = advance(g, states)
    else:
        lax.fori_loop(0, pieces, advance, states)

    cos_one, sin_one = outer[0], outer[1]
    bin_row = lax.broadcasted_iota(jnp.int32, (high, LANES), 0)
    bin_lane = lax.broadcasted_iota(jnp.int32, (high, LANES), 1)
    weight = jnp.where(bin_row + bin_lane == 0, 1.0 / length, 2.0 / length).astype(F32)
    top_row = lax.broadcasted_iota(jnp.int32, (rows, LANES), 0) == 0
    left = []
    for c in range(2):
        real, imag = [], []
        for i in range(near):
            scale = jnp.exp(-0.5 * logs[c, place + i]) * weight
            real.append(spec[c, place + i, :high] * scale)
            imag.append(spec[c, place + i, high : 2 * high] * scale)
        for i in range(near - 1):
            cos_parts, sin_parts = [], []
            for kh in range(high):
                re = jnp.broadcast_to(real[i][kh : kh + 1], (rows, LANES))
                im = jnp.broadcast_to(imag[i][kh : kh + 1], (rows, LANES))
                if i == 0:
                    re = jnp.where(top_row, real[near - 1][kh : kh + 1], re)
                    im = jnp.where(top_row, imag[near - 1][kh : kh + 1], im)
                cos_parts.append(re * cos_one + im * sin_one)
                sin_parts.append(im * cos_one - re * sin_one)
            left.append(jnp.concatenate(cos_parts + sin_parts, axis=1))
    white = product_two(jnp.concatenate(left, axis=0), full[...])
    white = white.astype(BF16).astype(F32)

    first_out = behind * rows - 1
    out_frames = rows + 2
    first_t = first_out - (lags - 1)
    t_frames = lags - 1 + out_frames
    assert first_t == rows and first_t + t_frames - 1 == (near - 1) * rows
    right = keep_right()

    def frame(c, s):
        at = c * (near - 1) * rows + (first_t + s) % ((near - 1) * rows)
        return circulant(white[at : at + 1])

    earlier = [
        circulant(white[top : top + 1])
        for top in (first_t - 1, (near - 1) * rows + first_t - 1)
    ]
    toeplitz = []
    for s in range(t_frames):
        tiles = []
        for c in range(2):
            now = frame(c, s)
            tiles.append(jnp.where(right, now, earlier[c]).astype(BF16))
            earlier[c] = now
        toeplitz.append(jnp.concatenate(tiles, axis=0))

    low_half = lax.broadcasted_iota(jnp.int32, (8, LANES), 0) < 4
    low_phase = lax.broadcasted_iota(jnp.int32, (8, LANES), 0) % 4 < 2
    after = jnp.where(place == pieces - 1, 0.0, 1.0).astype(F32)
    lane_row = lax.broadcasted_iota(jnp.int32, (LANES, LANES), 0)
    lane_col = lax.broadcasted_iota(jnp.int32, (LANES, LANES), 1)
    upto = (lane_row <= lane_col).astype(BF16)
    sums = jnp.concatenate([upto, jnp.ones((LANES, LANES), BF16)], axis=1)

    def conv(k):
        crossed = slots[k][1]
        parts = []
        for c in (crossed, 1 - crossed):
            ref, start = piece(c, k)
            top = start + tms * spec_rows + (c ^ crossed) * lag_rows
            parts.append(ref[top : top + lag_rows])
        return jnp.concatenate(parts, axis=1)

    def convolved(members):
        count = len(members)
        filt = [conv(d) for d in members]
        f_all = jnp.concatenate(
            [f[top : top + 16] for top in range(0, lag_rows, 16) for f in filt], axis=0
        )
        accs = [[None] * (out_frames + 1) for _ in members]
        for s in range(0, t_frames, 2):
            both = range(s, min(s + 2, t_frames))
            valid = [
                (a, t, t - (lags - 2) + 2 * a)
                for a in range(lags // 2)
                for t in both
                if 0 <= t - (lags - 2) + 2 * a <= out_frames
            ]
            low = min(a for a, _, _ in valid) // 2
            top = max(a for a, _, _ in valid) // 2 + 1
            g = jnp.dot(
                f_all[low * 16 * count : top * 16 * count],
                jnp.concatenate([toeplitz[t] for t in both], axis=1),
                preferred_element_type=F32,
            )
            for a, t, n in valid:
                for k in range(count):
                    row = ((a // 2 - low) * count + k) * 16 + a % 2 * 8
                    tile = g[row : row + 8, (t - s) * LANES : (t - s + 1) * LANES]
                    accs[k][n] = tile if accs[k][n] is None else accs[k][n] + tile
        return [
            [acc[n + 1] + pltpu.roll(acc[n], 4, 0) for n in range(out_frames)] for acc in accs
        ]

    def outputs(pair, z, corr, power, run):
        lag_now = jnp.where(low_half, lag[pair[0]], lag[pair[1]])
        for n in range(rows):
            tile = slice(8 * n, 8 * n + 8)
            c_re = jnp.where(low_half, corr[0][tile, :LANES], corr[1][tile, :LANES])
            c_im = jnp.where(low_half, corr[0][tile, LANES:], corr[1][tile, LANES:])
            mid = z[n + 1]
            turned = jnp.where(low_phase, -pltpu.roll(mid, 6, 0), pltpu.roll(mid, 2, 0))
            cross = mid * c_re + turned * c_im
            cross = cross + pltpu.roll(cross, 6, 0)
            here = slice(8 * n + 8, 8 * n + 16)
            after_it = slice(8 * n + 16, 8 * n + 24)
            win = (run[tile, LANES:] - run[tile, :LANES] + power[n]) + (
                run[here, LANES:] + run[after_it, :LANES]
            )
            energy = power[n + 1]
            chi = (win - 2.0 * cross + energy * lag_now) / (2 * window + 1)
            lanes = slice(n * LANES, (n + 1) * LANES)
            for top, member in zip((0, 4), pair):
                snr_out[member, :, lanes] = energy[top : top + 2]
                chi_out[member, :, lanes] = chi[top : top + 2]

    dims = (((1,), (1,)), ((), ()))
    for group in range(0, banks, 4):
        members = range(group, min(group + 4, banks))
        frames = convolved(members)
        z_all, power_all, pairs, corr_all = [], [], [], []
        for first in range(0, len(members), 2):
            pairs.append([bank ^ slots[k][0] for k in members[first : first + 2]])
            z0, z1 = frames[first], frames[first + 1]
            z = [jnp.where(low_half, p, pltpu.roll(q, 4, 0)) for p, q in zip(z0, z1)]
            z[-1] = z[-1] * after
            z_all.append(z)
        for z, pair in zip(z_all, pairs):
            stacked = jnp.concatenate(
                [jnp.concatenate(z[n : n + rows], axis=0) for n in range(3)], axis=1
            )
            up, low = split_two(stacked)
            both = jnp.concatenate([up, low], axis=0)
            count = up.shape[0]
            corr = []
            for member in pair:
                b_up = jnp.concatenate([band_up[member, d] for d in range(3)], axis=1)
                b_low = jnp.concatenate([band_low[member, d] for d in range(3)], axis=1)
                one = lax.dot_general(both, b_up, dims, preferred_element_type=F32)
                two = lax.dot_general(up, b_low, dims, preferred_element_type=F32)
                corr.append(one[:count] + one[count:] + two)
            corr_all.append(corr)
            squares = [v * v for v in z]
            power_all.append([v + pltpu.roll(v, 6, 0) for v in squares])
        stacked = jnp.concatenate([v for power in power_all for v in power], axis=0)
        up, low = split_two(stacked)
        run_all = jnp.dot(
            jnp.concatenate([up, low], axis=0), sums, preferred_element_type=F32
        )
        count = stacked.shape[0]
        run_all = run_all[:count] + run_all[count:]
        step = 8 * out_frames
        for k, pair in enumerate(pairs):
            run = run_all[k * step : (k + 1) * step]
            outputs(pair, z_all[k], corr_all[k], power_all[k], run)


ON_CHIP_BYTES = 3 * 2**20


def on_chip(*arrays):
    if sum(a.size * a.dtype.itemsize for a in arrays) > ON_CHIP_BYTES:
        return arrays
    return [pltpu.with_memory_space_constraint(a, pltpu.VMEM) for a in map(jnp.asarray, arrays)]


def on_chip_shape(shape, dtype):
    if 2 * math.prod(shape) * jnp.dtype(dtype).itemsize > ON_CHIP_BYTES:
        return jax.ShapeDtypeStruct(shape, dtype)
    return pltpu.VMEM(shape, dtype)


VMEM = pl.BlockSpec(memory_space=pltpu.VMEM)
SMEM = pl.BlockSpec(memory_space=pltpu.SMEM)


def body(
    strain, gate_mask, psd_reset, psd_ref, psd_rate, filters, basis_count, mixing, autocorrelation
):
    length = strain.shape[1]
    rows = length // LANES
    high = length // 2 // LANES
    banks = lax.axis_size("bank")
    tms = lax.axis_size("tm")
    basis, taps = filters.shape[2:]
    templ = mixing.shape[2]
    window = autocorrelation.shape[2] // 2
    lags = taps // LANES
    outer, shift, start, full = tables(length)

    spec = pl.pallas_call(
        spectrum_kernel,
        out_shape=pltpu.VMEM((8 * high, LANES), BF16),
        in_specs=[VMEM, VMEM, SMEM] + [VMEM] * 5,
        out_specs=VMEM,
        name="spectrum",
    )(
        strain.reshape(rows, LANES),
        gate_mask.reshape(rows, LANES),
        psd_reset,
        psd_ref.reshape(high, LANES),
        psd_rate.reshape(high, LANES),
        outer,
        shift,
        start,
    )
    combined = pl.pallas_call(
        filter_kernel,
        out_shape=pltpu.VMEM((2 * templ * lags, LANES), BF16),
        in_specs=[VMEM, VMEM, SMEM],
        out_specs=VMEM,
        name="filters",
    )(filters.reshape(basis, taps), mixing.reshape(2 * templ, basis), basis_count)
    band = on_chip_shape((banks, 3, 2 * LANES, LANES), BF16)
    band_up, band_low, lag = pl.pallas_call(
        band_kernel,
        out_shape=(band, band, pltpu.VMEM((banks, 8, LANES), F32)),
        in_specs=[VMEM],
        out_specs=(VMEM, VMEM, VMEM),
        name="bands",
    )(autocorrelation)

    distance = 1
    while distance < tms:
        spec = jnp.concatenate([spec, swapped(spec, "tm", distance)])
        distance *= 2
    held = jnp.concatenate([spec, combined])
    slots = [(0, 0)]
    distance = banks // 2
    while distance > 2:
        held = jnp.concatenate([held, swapped(held, "bank", distance)])
        slots = slots + [(d ^ distance, p ^ 1) for d, p in slots]
        distance //= 2
    far = swapped(held, "bank", 2)
    near = swapped(held, "bank", 1)
    first = jnp.concatenate([held, near])
    last = swapped(far, "bank", 1)
    second = jnp.concatenate([far, last])
    slots = slots + [(d ^ 1, p ^ 1) for d, p in slots]
    slots = slots + [(d ^ 2, p ^ 1) for d, p in slots]
    first_other = swapped_cores(first)
    second_other = swapped_cores(second)

    behind = -(-(taps + window) // length)
    near = behind + 2
    share = templ // 2
    out = jax.ShapeDtypeStruct((banks, share, length), F32)
    return pl.pallas_call(
        functools.partial(
            output_kernel, slots=slots, tms=tms, length=length, taps=taps, window=window
        ),
        out_shape=(out, out),
        in_specs=[VMEM] * 9,
        out_specs=(VMEM, VMEM),
        scratch_shapes=[
            pltpu.VMEM((2, banks * tms + behind + 1, 4 * high, LANES), F32),
            pltpu.VMEM((2, banks * tms + behind + 1, high, LANES), F32),
        ],
        name="outputs",
    )(*on_chip(first, second, first_other, second_other, full, outer, band_up, band_low, lag))


def solution(mesh):
    return jax.shard_map(
        body,
        mesh=mesh,
        in_specs=(
            P("rate", ("parts", "bank", "tm")),
            P(("parts", "bank", "tm")),
            P(("parts", "bank", "tm")),
            P("rate", None),
            P("rate", None),
            P("bank", "rate", None, None),
            P("bank"),
            P("bank", "rate", None, None, None),
            P(),
        ),
        out_specs=(
            P(None, "rate", ("parts", "bank", "tm")),
            P(None, "rate", ("parts", "bank", "tm")),
        ),
        check_vma=False,
    )
```

```python
import functools
import math

import jax
import jax.numpy as jnp
import numpy as np
from jax import lax
from jax.experimental import pallas as pl
from jax.experimental.pallas import tpu as pltpu
from jax.sharding import PartitionSpec as P


LANES = 128
F32 = jnp.float32
BF16 = jnp.bfloat16


def swapped(block, axis, distance):
    count = lax.axis_size("rate")
    places = range(lax.axis_size(axis) * count)
    route = [(i, (i // count ^ distance) * count + (i % count ^ 1)) for i in places]
    return lax.ppermute(block, (axis, "rate"), route)


def swapped_cores(block):
    return lax.ppermute(block, "rate", [(i, i ^ 1) for i in range(lax.axis_size("rate"))])


def two_terms(table):
    upper = table.astype(BF16)
    return upper, (table - upper.astype(np.float32)).astype(BF16)


def tables(length):
    rows = length // LANES
    high = length // 2 // LANES
    lane = np.arange(LANES)
    turn = 2.0 * math.pi
    outer = turn * (np.arange(rows)[:, None] * lane[None, :] % rows) / rows
    outer = np.stack([np.cos(outer), np.sin(outer)])
    shift = turn * (np.arange(high)[:, None] * lane[None, :] % rows) / rows
    shift = np.stack([np.cos(shift), np.sin(shift)])
    step = 8
    fine = turn * (np.arange(step)[:, None] * lane[None, :]) / length
    coarse = turn * (np.arange(0, LANES, step)[:, None] * lane[None, :]) / length
    start = np.concatenate([np.cos(fine), np.sin(fine), np.cos(coarse), np.sin(coarse)])
    bins = np.arange(length // 2)
    full = turn * (bins[:, None] * lane[None, :] % length) / length
    full = np.concatenate([np.cos(full), np.sin(full)], axis=0)
    outer, shift, start, full = (a.astype(np.float32) for a in (outer, shift, start, full))
    return outer, shift, start, np.concatenate(two_terms(full), axis=1)


def split_two(value):
    upper = value.astype(BF16)
    return upper, (value - upper.astype(F32)).astype(BF16)


def product_two(left, right):
    upper, lower = split_two(left)
    count, width = left.shape[0], right.shape[1] // 2
    both = jnp.dot(jnp.concatenate([upper, lower], axis=0), right, preferred_element_type=F32)
    small = (both[:count, width:] + both[count:, width:]) + both[count:, :width]
    return both[:count, :width] + small


def circulant(row):
    return pltpu.roll(jnp.broadcast_to(row, (LANES, LANES)), 0, 1, stride=1, stride_axis=0)


def keep_right():
    u = lax.broadcasted_iota(jnp.int32, (LANES, LANES), 0)
    q = lax.broadcasted_iota(jnp.int32, (LANES, LANES), 1)
    return q >= u


def spectrum_kernel(strain, mask, reset, psd_ref, psd_rate, outer, shift, start, out, levels):
    rows = strain.shape[0]
    high = psd_ref.shape[0]
    levels[:high] = psd_ref[...]
    levels[high:] = psd_rate[...]
    signal = strain[...] * mask[...].astype(F32)
    step = start.shape[0] // 2 - LANES // 8
    fine_c, fine_s = start[:step], start[step : 2 * step]
    wide_c, wide_s = start[2 * step : 2 * step + LANES // 8], start[2 * step + LANES // 8 :]
    cos_rows, sin_rows = [], []
    for a in range(LANES // 8):
        c, s = wide_c[a : a + 1], wide_s[a : a + 1]
        cos_rows.append(c * fine_c - s * fine_s)
        sin_rows.append(s * fine_c + c * fine_s)
    cos_all, sin_all = jnp.concatenate(cos_rows, axis=0), jnp.concatenate(sin_rows, axis=0)
    terms = [split_two(v) for v in (cos_all, sin_all)]
    inner = jnp.concatenate([terms[0][0], terms[1][0], terms[0][1], terms[1][1]], axis=1)
    left = [signal * shift[i, k : k + 1] for i in range(2) for k in range(high)]
    product = product_two(jnp.concatenate(left, axis=0), inner)
    cos_one, sin_one = outer[0], outer[1]
    real_rows, imag_rows = [], []
    for kh in range(high):
        with_cos = product[kh * rows : (kh + 1) * rows]
        with_sin = product[(high + kh) * rows : (high + kh + 1) * rows]
        cos_sum = with_cos[:, :LANES] - with_sin[:, LANES:]
        sin_sum = with_cos[:, LANES:] + with_sin[:, :LANES]
        real_rows.append(jnp.sum(cos_one * cos_sum - sin_one * sin_sum, axis=0, keepdims=True))
        imag_rows.append(jnp.sum(sin_one * cos_sum + cos_one * sin_sum, axis=0, keepdims=True))
    real_part = jnp.concatenate(real_rows, axis=0)
    imag_part = jnp.concatenate(imag_rows, axis=0)
    row = lax.broadcasted_iota(jnp.int32, imag_part.shape, 0)
    lane = lax.broadcasted_iota(jnp.int32, imag_part.shape, 1)
    imag_part = jnp.where(row + lane == 0, reset[0].astype(F32), imag_part)
    upper, lower = split_two(jnp.concatenate([real_part, imag_part], axis=0))
    out[: 2 * high] = upper
    out[2 * high :] = lower


def filter_kernel(filters, mixing, count, out):
    total, basis = mixing.shape
    share = total // 2
    templ = share // 2
    rate = lax.axis_index("rate")
    row = lax.broadcasted_iota(jnp.int32, (total, total), 0)
    col = lax.broadcasted_iota(jnp.int32, (total, total), 1)
    part = (row // share) ^ rate
    source = (part * templ + row % templ) * 2 + row % share // templ
    choose = (col == source).astype(BF16)
    ordered = jnp.dot(choose, mixing[...], preferred_element_type=F32)
    live = lax.broadcasted_iota(jnp.int32, (total, basis), 1) < count[0]
    ordered = jnp.where(live, ordered, 0.0).astype(BF16)
    combined = jnp.dot(ordered, filters[...], preferred_element_type=F32)
    lags = filters.shape[1] // LANES
    low_half = lax.broadcasted_iota(jnp.int32, (total, LANES), 0) < share
    own, other = [], []
    for a in range(0, lags, 2):
        even = combined[:, a * LANES : (a + 1) * LANES]
        odd = combined[:, (a + 1) * LANES : (a + 2) * LANES]
        own.append(jnp.where(low_half, even, pltpu.roll(odd, share, 0)))
        other.append(jnp.where(low_half, pltpu.roll(even, share, 0), odd))
    out[...] = jnp.concatenate(own + other, axis=0).astype(BF16)


def band_kernel(series, levels, levels_other, upper_out, lower_out, lag_out, levels_out):
    high = levels.shape[0] // 2
    for c, ref in enumerate((levels, levels_other)):
        reference_psd, rate = ref[:high], ref[high:]
        for k, value in enumerate((0.1 * reference_psd, jnp.log(reference_psd), rate)):
            levels_out[c, k] = jnp.concatenate([value, value], axis=0)
    right = keep_right()
    for b in range(series.shape[0]):
        lag = jnp.zeros((1, 1), F32)
        for part in range(2):
            row = series[b, part : part + 1, :]
            lag = lag + jnp.sum(row * row, axis=1, keepdims=True)
            fill = jnp.zeros((1, 3 * LANES - row.shape[1]), F32)
            row = jnp.concatenate([row, fill], axis=1)
            before = jnp.zeros((LANES, LANES), F32)
            for d in range(3):
                now = circulant(row[:, d * LANES : (d + 1) * LANES])
                upper, lower = split_two(jnp.where(right, now, before))
                upper_out[b, d, part * LANES : (part + 1) * LANES] = upper
                lower_out[b, d, part * LANES : (part + 1) * LANES] = lower
                before = now
        lag_out[b] = jnp.broadcast_to(lag, (8, LANES))


def output_kernel(
    own_a, own_b, other_a, other_b, full, outer, band_up, band_low, lag, levels,
    snr_out, chi_out, spec, drives, keeps, logs, *, slots, tms, length, taps, window,
):
    rows = length // LANES
    high = length // 2 // LANES
    spec_rows = 4 * high
    lags = taps // LANES
    lag_rows = lags * 4
    piece_rows = tms * spec_rows + 2 * lag_rows
    pieces = len(slots) * tms
    behind = -(-(taps + window) // length)
    near = behind + 2
    banks = len(slots)
    half = banks // 2
    bank = lax.axis_index("bank")
    tm = lax.axis_index("tm")
    place = bank * tms + tm
    bufs = ((own_a, own_b), (other_a, other_b))

    def piece(c, d):
        return bufs[c][d // half], (d % half) * piece_rows

    tile_row = lax.broadcasted_iota(jnp.int32, (2 * high, LANES), 0)
    tile_lane = lax.broadcasted_iota(jnp.int32, (2 * high, LANES), 1)
    flag_place = (tile_row == high) & (tile_lane == 0)
    zero = jnp.zeros((2 * high, LANES), F32)
    for c in range(2):
        for i in range(behind):
            spec[c, i] = zero
            logs[c, i] = zero
        spec[c, pieces + behind] = zero
        logs[c, pieces + behind] = zero
        for k, (d, crossed) in enumerate(slots):
            ref, start = piece(c, k)
            for e in range(tms):
                top = start + e * spec_rows
                value = ref[top : top + 2 * high].astype(F32)
                value = value + ref[top + 2 * high : top + 4 * high].astype(F32)
                band = c ^ crossed ^ (e.bit_count() & 1)
                at = (bank ^ d) * tms + (tm ^ e)
                flag = value[high : high + 1, 0:1]
                value = jnp.where(flag_place, 0.0, value)
                square = value * value
                power = (square + pltpu.roll(square, high, 0)) / (length / 2)
                rate = levels[band, 2]
                spec[band, at + behind] = value
                drives[band, at] = rate * jnp.log(power + levels[band, 0])
                keeps[band, at] = (1.0 - rate) * (1.0 - 0.5 * flag)

    def advance(g, states):
        nexts = []
        for c in range(2):
            nexts.append(keeps[c, g] * states[c] + drives[c, g])
            logs[c, g + behind] = nexts[c]
        return tuple(nexts)

    states = (levels[0, 1], levels[1, 1])
    if pieces <= 16:
        for g in range(pieces):
            states = advance(g, states)
    else:
        lax.fori_loop(0, pieces, advance, states)

    cos_one, sin_one = outer[0], outer[1]
    first_bin = (tile_row % high == 0) & (tile_lane == 0)
    weight = jnp.where(first_bin, 1.0 / length, 2.0 / length).astype(F32)
    top_row = lax.broadcasted_iota(jnp.int32, (rows, LANES), 0) == 0
    left = []
    for c in range(2):
        real, imag = [], []
        for i in range(near):
            scaled = spec[c, place + i] * (jnp.exp(-0.5 * logs[c, place + i]) * weight)
            real.append(scaled[:high])
            imag.append(scaled[high:])
        for i in range(near - 1):
            cos_parts, sin_parts = [], []
            for kh in range(high):
                re = jnp.broadcast_to(real[i][kh : kh + 1], (rows, LANES))
                im = jnp.broadcast_to(imag[i][kh : kh + 1], (rows, LANES))
                if i == 0:
                    re = jnp.where(top_row, real[near - 1][kh : kh + 1], re)
                    im = jnp.where(top_row, imag[near - 1][kh : kh + 1], im)
                cos_parts.append(re * cos_one + im * sin_one)
                sin_parts.append(im * cos_one - re * sin_one)
            left.append(jnp.concatenate(cos_parts + sin_parts, axis=1))
    white = product_two(jnp.concatenate(left, axis=0), full[...])
    white = white.astype(BF16).astype(F32)

    first_out = behind * rows - 1
    out_frames = rows + 2
    first_t = first_out - (lags - 1)
    t_frames = lags - 1 + out_frames
    assert first_t == rows and first_t + t_frames - 1 == (near - 1) * rows
    right = keep_right()

    def frame(c, s):
        at = c * (near - 1) * rows + (first_t + s) % ((near - 1) * rows)
        return circulant(white[at : at + 1])

    earlier = [
        circulant(white[top : top + 1])
        for top in (first_t - 1, (near - 1) * rows + first_t - 1)
    ]
    toeplitz = []
    for s in range(t_frames):
        tiles = []
        for c in range(2):
            now = frame(c, s)
            tiles.append(jnp.where(right, now, earlier[c]).astype(BF16))
            earlier[c] = now
        toeplitz.append(jnp.concatenate(tiles, axis=0))

    low_half = lax.broadcasted_iota(jnp.int32, (8, LANES), 0) < 4
    low_phase = lax.broadcasted_iota(jnp.int32, (8, LANES), 0) % 4 < 2
    after = jnp.where(place == pieces - 1, 0.0, 1.0).astype(F32)
    lane_row = lax.broadcasted_iota(jnp.int32, (LANES, LANES), 0)
    lane_col = lax.broadcasted_iota(jnp.int32, (LANES, LANES), 1)
    upto = (lane_row <= lane_col).astype(BF16)
    sums = jnp.concatenate([upto, jnp.ones((LANES, LANES), BF16)], axis=1)

    def conv(k):
        crossed = slots[k][1]
        parts = []
        for c in (crossed, 1 - crossed):
            ref, start = piece(c, k)
            top = start + tms * spec_rows + (c ^ crossed) * lag_rows
            parts.append(ref[top : top + lag_rows])
        return jnp.concatenate(parts, axis=1)

    def convolved(members):
        count = len(members)
        filt = [conv(d) for d in members]
        f_all = jnp.concatenate(
            [f[top : top + 16] for top in range(0, lag_rows, 16) for f in filt], axis=0
        )
        accs = [[None] * (out_frames + 1) for _ in members]
        for s in range(0, t_frames, 2):
            both = range(s, min(s + 2, t_frames))
            valid = [
                (a, t, t - (lags - 2) + 2 * a)
                for a in range(lags // 2)
                for t in both
                if 0 <= t - (lags - 2) + 2 * a <= out_frames
            ]
            low = min(a for a, _, _ in valid) // 2
            top = max(a for a, _, _ in valid) // 2 + 1
            g = jnp.dot(
                f_all[low * 16 * count : top * 16 * count],
                jnp.concatenate([toeplitz[t] for t in both], axis=1),
                preferred_element_type=F32,
            )
            for a, t, n in valid:
                for k in range(count):
                    row = ((a // 2 - low) * count + k) * 16 + a % 2 * 8
                    tile = g[row : row + 8, (t - s) * LANES : (t - s + 1) * LANES]
                    accs[k][n] = tile if accs[k][n] is None else accs[k][n] + tile
        return [
            [acc[n + 1] + pltpu.roll(acc[n], 4, 0) for n in range(out_frames)] for acc in accs
        ]

    def outputs(pair, z, corr, power, run):
        lag_now = jnp.where(low_half, lag[pair[0]], lag[pair[1]])
        for n in range(rows):
            tile = slice(8 * n, 8 * n + 8)
            c_re = jnp.where(low_half, corr[0][tile, :LANES], corr[1][tile, :LANES])
            c_im = jnp.where(low_half, corr[0][tile, LANES:], corr[1][tile, LANES:])
            mid = z[n + 1]
            turned = jnp.where(low_phase, -pltpu.roll(mid, 6, 0), pltpu.roll(mid, 2, 0))
            cross = mid * c_re + turned * c_im
            cross = cross + pltpu.roll(cross, 6, 0)
            here = slice(8 * n + 8, 8 * n + 16)
            after_it = slice(8 * n + 16, 8 * n + 24)
            win = (run[tile, LANES:] - run[tile, :LANES] + power[n]) + (
                run[here, LANES:] + run[after_it, :LANES]
            )
            energy = power[n + 1]
            chi = (win - 2.0 * cross + energy * lag_now) / (2 * window + 1)
            lanes = slice(n * LANES, (n + 1) * LANES)
            for top, member in zip((0, 4), pair):
                snr_out[member, :, lanes] = energy[top : top + 2]
                chi_out[member, :, lanes] = chi[top : top + 2]

    dims = (((1,), (1,)), ((), ()))
    for group in range(0, banks, 4):
        members = range(group, min(group + 4, banks))
        frames = convolved(members)
        z_all, power_all, pairs, corr_all = [], [], [], []
        for first in range(0, len(members), 2):
            pairs.append([bank ^ slots[k][0] for k in members[first : first + 2]])
            z0, z1 = frames[first], frames[first + 1]
            z = [jnp.where(low_half, p, pltpu.roll(q, 4, 0)) for p, q in zip(z0, z1)]
            z[-1] = z[-1] * after
            z_all.append(z)
        for z, pair in zip(z_all, pairs):
            stacked = jnp.concatenate(
                [jnp.concatenate(z[n : n + rows], axis=0) for n in range(3)], axis=1
            )
            up, low = split_two(stacked)
            both = jnp.concatenate([up, low], axis=0)
            count = up.shape[0]
            corr = []
            for member in pair:
                b_up = jnp.concatenate([band_up[member, d] for d in range(3)], axis=1)
                b_low = jnp.concatenate([band_low[member, d] for d in range(3)], axis=1)
                one = lax.dot_general(both, b_up, dims, preferred_element_type=F32)
                two = lax.dot_general(up, b_low, dims, preferred_element_type=F32)
                corr.append(one[:count] + one[count:] + two)
            corr_all.append(corr)
            squares = [v * v for v in z]
            power_all.append([v + pltpu.roll(v, 6, 0) for v in squares])
        stacked = jnp.concatenate([v for power in power_all for v in power], axis=0)
        up, low = split_two(stacked)
        run_all = jnp.dot(
            jnp.concatenate([up, low], axis=0), sums, preferred_element_type=F32
        )
        count = stacked.shape[0]
        run_all = run_all[:count] + run_all[count:]
        step = 8 * out_frames
        for k, pair in enumerate(pairs):
            run = run_all[k * step : (k + 1) * step]
            outputs(pair, z_all[k], corr_all[k], power_all[k], run)


ON_CHIP_BYTES = 3 * 2**20


def on_chip(*arrays):
    if sum(a.size * a.dtype.itemsize for a in arrays) > ON_CHIP_BYTES:
        return arrays
    return [pltpu.with_memory_space_constraint(a, pltpu.VMEM) for a in map(jnp.asarray, arrays)]


def on_chip_shape(shape, dtype):
    if 2 * math.prod(shape) * jnp.dtype(dtype).itemsize > ON_CHIP_BYTES:
        return jax.ShapeDtypeStruct(shape, dtype)
    return pltpu.VMEM(shape, dtype)


VMEM = pl.BlockSpec(memory_space=pltpu.VMEM)
SMEM = pl.BlockSpec(memory_space=pltpu.SMEM)


def body(
    strain, gate_mask, psd_reset, psd_ref, psd_rate, filters, basis_count, mixing, autocorrelation
):
    length = strain.shape[1]
    rows = length // LANES
    high = length // 2 // LANES
    banks = lax.axis_size("bank")
    tms = lax.axis_size("tm")
    basis, taps = filters.shape[2:]
    templ = mixing.shape[2]
    window = autocorrelation.shape[2] // 2
    lags = taps // LANES
    outer, shift, start, full = tables(length)

    spec, levels = pl.pallas_call(
        spectrum_kernel,
        out_shape=(
            pltpu.VMEM((4 * high, LANES), BF16),
            pltpu.VMEM((2 * high, LANES), F32),
        ),
        in_specs=[VMEM, VMEM, SMEM] + [VMEM] * 5,
        out_specs=(VMEM, VMEM),
        name="spectrum",
    )(
        strain.reshape(rows, LANES),
        gate_mask.reshape(rows, LANES),
        psd_reset,
        psd_ref.reshape(high, LANES),
        psd_rate.reshape(high, LANES),
        outer,
        shift,
        start,
    )
    combined = pl.pallas_call(
        filter_kernel,
        out_shape=pltpu.VMEM((2 * templ * lags, LANES), BF16),
        in_specs=[VMEM, VMEM, SMEM],
        out_specs=VMEM,
        name="filters",
    )(filters.reshape(basis, taps), mixing.reshape(2 * templ, basis), basis_count)
    distance = 1
    while distance < tms:
        spec = jnp.concatenate([spec, swapped(spec, "tm", distance)])
        distance *= 2
    held = jnp.concatenate([spec, combined])
    slots = [(0, 0)]
    distance = banks // 2
    while distance > 2:
        held = jnp.concatenate([held, swapped(held, "bank", distance)])
        slots = slots + [(d ^ distance, p ^ 1) for d, p in slots]
        distance //= 2
    far = swapped(held, "bank", 2)
    near = swapped(held, "bank", 1)
    first = jnp.concatenate([held, near])
    levels_other = swapped_cores(levels)
    last = swapped(far, "bank", 1)
    second = jnp.concatenate([far, last])
    slots = slots + [(d ^ 1, p ^ 1) for d, p in slots]
    slots = slots + [(d ^ 2, p ^ 1) for d, p in slots]
    first_other = swapped_cores(first)
    second_other = swapped_cores(second)

    band = on_chip_shape((banks, 3, 2 * LANES, LANES), BF16)
    band_up, band_low, lag, levels = pl.pallas_call(
        band_kernel,
        out_shape=(
            band,
            band,
            pltpu.VMEM((banks, 8, LANES), F32),
            pltpu.VMEM((2, 3, 2 * high, LANES), F32),
        ),
        in_specs=[VMEM] * 3,
        out_specs=(VMEM,) * 4,
        name="bands",
    )(autocorrelation, *on_chip(levels, levels_other))

    behind = -(-(taps + window) // length)
    near = behind + 2
    share = templ // 2
    out = jax.ShapeDtypeStruct((banks, share, length), F32)
    return pl.pallas_call(
        functools.partial(
            output_kernel, slots=slots, tms=tms, length=length, taps=taps, window=window
        ),
        out_shape=(out, out),
        in_specs=[VMEM] * 10,
        out_specs=(VMEM, VMEM),
        scratch_shapes=[
            pltpu.VMEM((2, banks * tms + behind + 1, 2 * high, LANES), F32),
            pltpu.VMEM((2, banks * tms, 2 * high, LANES), F32),
            pltpu.VMEM((2, banks * tms, 2 * high, LANES), F32),
            pltpu.VMEM((2, banks * tms + behind + 1, 2 * high, LANES), F32),
        ],
        name="outputs",
    )(*on_chip(first, second, first_other, second_other, full, outer, band_up, band_low, lag, levels))


def solution(mesh):
    return jax.shard_map(
        body,
        mesh=mesh,
        in_specs=(
            P("rate", ("parts", "bank", "tm")),
            P(("parts", "bank", "tm")),
            P(("parts", "bank", "tm")),
            P("rate", None),
            P("rate", None),
            P("bank", "rate", None, None),
            P("bank"),
            P("bank", "rate", None, None, None),
            P(),
        ),
        out_specs=(
            P(None, "rate", ("parts", "bank", "tm")),
            P(None, "rate", ("parts", "bank", "tm")),
        ),
        check_vma=False,
    )
```

```python
import functools
import math

import jax
import jax.numpy as jnp
import numpy as np
from jax import lax
from jax.experimental import pallas as pl
from jax.experimental.pallas import tpu as pltpu
from jax.sharding import PartitionSpec as P


LANES = 128
F32 = jnp.float32
BF16 = jnp.bfloat16


def swapped(block, axis, distance):
    count = lax.axis_size("rate")
    places = range(lax.axis_size(axis) * count)
    route = [(i, (i // count ^ distance) * count + (i % count ^ 1)) for i in places]
    return lax.ppermute(block, (axis, "rate"), route)


def swapped_cores(block):
    return lax.ppermute(block, "rate", [(i, i ^ 1) for i in range(lax.axis_size("rate"))])


def two_terms(table):
    upper = table.astype(BF16)
    return upper, (table - upper.astype(np.float32)).astype(BF16)


def tables(length):
    rows = length // LANES
    high = length // 2 // LANES
    lane = np.arange(LANES)
    turn = 2.0 * math.pi
    outer = turn * (np.arange(rows)[:, None] * lane[None, :] % rows) / rows
    outer = np.stack([np.cos(outer), np.sin(outer)])
    shift = turn * (np.arange(high)[:, None] * lane[None, :] % rows) / rows
    shift = np.stack([np.cos(shift), np.sin(shift)])
    step = 8
    fine = turn * (np.arange(step)[:, None] * lane[None, :]) / length
    coarse = turn * (np.arange(0, LANES, step)[:, None] * lane[None, :]) / length
    start = np.concatenate([np.cos(fine), np.sin(fine), np.cos(coarse), np.sin(coarse)])
    bins = np.arange(length // 2)
    full = turn * (bins[:, None] * lane[None, :] % length) / length
    full = np.concatenate([np.cos(full), np.sin(full)], axis=0)
    outer, shift, start, full = (a.astype(np.float32) for a in (outer, shift, start, full))
    return outer, shift, start, np.concatenate(two_terms(full), axis=1)


def split_two(value):
    upper = value.astype(BF16)
    return upper, (value - upper.astype(F32)).astype(BF16)


def product_two(left, right):
    upper, lower = split_two(left)
    count, width = left.shape[0], right.shape[1] // 2
    both = jnp.dot(jnp.concatenate([upper, lower], axis=0), right, preferred_element_type=F32)
    small = (both[:count, width:] + both[count:, width:]) + both[count:, :width]
    return both[:count, :width] + small


def circulant(row):
    return pltpu.roll(jnp.broadcast_to(row, (LANES, LANES)), 0, 1, stride=1, stride_axis=0)


def keep_right():
    u = lax.broadcasted_iota(jnp.int32, (LANES, LANES), 0)
    q = lax.broadcasted_iota(jnp.int32, (LANES, LANES), 1)
    return q >= u


def spectrum_kernel(strain, mask, reset, psd_ref, psd_rate, outer, shift, start, out, levels):
    rows = strain.shape[0]
    high = psd_ref.shape[0]
    levels[:high] = psd_ref[...]
    levels[high:] = psd_rate[...]
    signal = strain[...] * mask[...].astype(F32)
    step = start.shape[0] // 2 - LANES // 8
    fine_c, fine_s = start[:step], start[step : 2 * step]
    wide_c, wide_s = start[2 * step : 2 * step + LANES // 8], start[2 * step + LANES // 8 :]
    cos_rows, sin_rows = [], []
    for a in range(LANES // 8):
        c, s = wide_c[a : a + 1], wide_s[a : a + 1]
        cos_rows.append(c * fine_c - s * fine_s)
        sin_rows.append(s * fine_c + c * fine_s)
    cos_all, sin_all = jnp.concatenate(cos_rows, axis=0), jnp.concatenate(sin_rows, axis=0)
    terms = [split_two(v) for v in (cos_all, sin_all)]
    inner = jnp.concatenate([terms[0][0], terms[1][0], terms[0][1], terms[1][1]], axis=1)
    left = [signal * shift[i, k : k + 1] for i in range(2) for k in range(high)]
    product = product_two(jnp.concatenate(left, axis=0), inner)
    cos_one, sin_one = outer[0], outer[1]
    real_rows, imag_rows = [], []
    for kh in range(high):
        with_cos = product[kh * rows : (kh + 1) * rows]
        with_sin = product[(high + kh) * rows : (high + kh + 1) * rows]
        cos_sum = with_cos[:, :LANES] - with_sin[:, LANES:]
        sin_sum = with_cos[:, LANES:] + with_sin[:, :LANES]
        real_rows.append(jnp.sum(cos_one * cos_sum - sin_one * sin_sum, axis=0, keepdims=True))
        imag_rows.append(jnp.sum(sin_one * cos_sum + cos_one * sin_sum, axis=0, keepdims=True))
    real_part = jnp.concatenate(real_rows, axis=0)
    imag_part = jnp.concatenate(imag_rows, axis=0)
    row = lax.broadcasted_iota(jnp.int32, imag_part.shape, 0)
    lane = lax.broadcasted_iota(jnp.int32, imag_part.shape, 1)
    imag_part = jnp.where(row + lane == 0, reset[0].astype(F32), imag_part)
    upper, lower = split_two(jnp.concatenate([real_part, imag_part], axis=0))
    out[: 2 * high] = upper
    out[2 * high :] = lower


def filter_kernel(filters, mixing, count, out):
    total, basis = mixing.shape
    share = total // 2
    templ = share // 2
    rate = lax.axis_index("rate")
    row = lax.broadcasted_iota(jnp.int32, (total, total), 0)
    col = lax.broadcasted_iota(jnp.int32, (total, total), 1)
    part = (row // share) ^ rate
    source = (part * templ + row % templ) * 2 + row % share // templ
    choose = (col == source).astype(BF16)
    ordered = jnp.dot(choose, mixing[...], preferred_element_type=F32)
    live = lax.broadcasted_iota(jnp.int32, (total, basis), 1) < count[0]
    ordered = jnp.where(live, ordered, 0.0).astype(BF16)
    combined = jnp.dot(ordered, filters[...], preferred_element_type=F32)
    lags = filters.shape[1] // LANES
    low_half = lax.broadcasted_iota(jnp.int32, (total, LANES), 0) < share
    own, other = [], []
    for a in range(0, lags, 2):
        even = combined[:, a * LANES : (a + 1) * LANES]
        odd = combined[:, (a + 1) * LANES : (a + 2) * LANES]
        own.append(jnp.where(low_half, even, pltpu.roll(odd, share, 0)))
        other.append(jnp.where(low_half, pltpu.roll(even, share, 0), odd))
    out[...] = jnp.concatenate(own + other, axis=0).astype(BF16)


def band_kernel(series, levels, levels_other, upper_out, lower_out, lag_out, levels_out):
    high = levels.shape[0] // 2
    for c, ref in enumerate((levels, levels_other)):
        reference_psd, rate = ref[:high], ref[high:]
        for k, value in enumerate((0.1 * reference_psd, jnp.log(reference_psd), rate)):
            levels_out[c, k] = jnp.concatenate([value, value], axis=0)
    right = keep_right()
    for b in range(series.shape[0]):
        lag = jnp.zeros((1, 1), F32)
        for part in range(2):
            row = series[b, part : part + 1, :]
            lag = lag + jnp.sum(row * row, axis=1, keepdims=True)
            fill = jnp.zeros((1, 3 * LANES - row.shape[1]), F32)
            row = jnp.concatenate([row, fill], axis=1)
            before = jnp.zeros((LANES, LANES), F32)
            for d in range(3):
                now = circulant(row[:, d * LANES : (d + 1) * LANES])
                upper, lower = split_two(jnp.where(right, now, before))
                upper_out[b, d, part * LANES : (part + 1) * LANES] = upper
                lower_out[b, d, part * LANES : (part + 1) * LANES] = lower
                before = now
        lag_out[b] = jnp.broadcast_to(lag, (8, LANES))


def output_kernel(
    own_a, own_b, other_a, other_b, full, outer, band_up, band_low, lag, levels,
    snr_out, chi_out, spec, drives, keeps, logs, *, slots, tms, length, taps, window,
):
    rows = length // LANES
    high = length // 2 // LANES
    spec_rows = 4 * high
    lags = taps // LANES
    lag_rows = lags * 4
    piece_rows = tms * spec_rows + 2 * lag_rows
    pieces = len(slots) * tms
    behind = -(-(taps + window) // length)
    near = behind + 2
    banks = len(slots)
    half = banks // 2
    bank = lax.axis_index("bank")
    tm = lax.axis_index("tm")
    place = bank * tms + tm
    bufs = ((own_a, own_b), (other_a, other_b))

    def piece(c, d):
        return bufs[c][d // half], (d % half) * piece_rows

    tile_row = lax.broadcasted_iota(jnp.int32, (2 * high, LANES), 0)
    tile_lane = lax.broadcasted_iota(jnp.int32, (2 * high, LANES), 1)
    flag_place = (tile_row == high) & (tile_lane == 0)
    zero = jnp.zeros((2 * high, LANES), F32)
    for c in range(2):
        for i in range(behind):
            spec[c, i] = zero
            logs[c, i] = zero
        spec[c, pieces + behind] = zero
        logs[c, pieces + behind] = zero
        for k, (d, crossed) in enumerate(slots):
            ref, start = piece(c, k)
            for e in range(tms):
                top = start + e * spec_rows
                value = ref[top : top + 2 * high].astype(F32)
                value = value + ref[top + 2 * high : top + 4 * high].astype(F32)
                band = c ^ crossed ^ (e.bit_count() & 1)
                at = (bank ^ d) * tms + (tm ^ e)
                flag = value[high : high + 1, 0:1]
                value = jnp.where(flag_place, 0.0, value)
                square = value * value
                power = (square + pltpu.roll(square, high, 0)) / (length / 2)
                rate = levels[band, 2]
                spec[band, at + behind] = value
                drives[band, at] = rate * jnp.log(power + levels[band, 0])
                keeps[band, at] = (1.0 - rate) * (1.0 - 0.5 * flag)

    def advance(g, states):
        nexts = []
        for c in range(2):
            nexts.append(keeps[c, g] * states[c] + drives[c, g])
            logs[c, g + behind] = nexts[c]
        return tuple(nexts)

    states = (levels[0, 1], levels[1, 1])
    if pieces <= 16:
        for g in range(pieces):
            states = advance(g, states)
    else:
        lax.fori_loop(0, pieces, advance, states)

    cos_one, sin_one = outer[0], outer[1]
    first_bin = (tile_row % high == 0) & (tile_lane == 0)
    weight = jnp.where(first_bin, 1.0 / length, 2.0 / length).astype(F32)
    top_row = lax.broadcasted_iota(jnp.int32, (rows, LANES), 0) == 0
    left = []
    for c in range(2):
        real, imag = [], []
        for i in range(near):
            scaled = spec[c, place + i] * (jnp.exp(-0.5 * logs[c, place + i]) * weight)
            real.append(scaled[:high])
            imag.append(scaled[high:])
        for i in range(near - 1):
            cos_parts, sin_parts = [], []
            for kh in range(high):
                re = jnp.broadcast_to(real[i][kh : kh + 1], (rows, LANES))
                im = jnp.broadcast_to(imag[i][kh : kh + 1], (rows, LANES))
                if i == 0:
                    re = jnp.where(top_row, real[near - 1][kh : kh + 1], re)
                    im = jnp.where(top_row, imag[near - 1][kh : kh + 1], im)
                cos_parts.append(re * cos_one + im * sin_one)
                sin_parts.append(im * cos_one - re * sin_one)
            left.append(jnp.concatenate(cos_parts + sin_parts, axis=1))
    white = product_two(jnp.concatenate(left, axis=0), full[...])
    white = white.astype(BF16).astype(F32)

    first_out = behind * rows - 1
    out_frames = rows + 2
    first_t = first_out - (lags - 1)
    t_frames = lags - 1 + out_frames
    assert first_t == rows and first_t + t_frames - 1 == (near - 1) * rows
    step = 16
    u_row = lax.broadcasted_iota(jnp.int32, (step, LANES), 0)
    q_lane = lax.broadcasted_iota(jnp.int32, (step, LANES), 1)
    rights = [q_lane >= u_row + top for top in range(0, LANES, step)]

    def turned(row):
        whole = circulant(row).astype(BF16)
        return [whole[top : top + step] for top in range(0, LANES, step)]

    def frame(c, s):
        at = c * (near - 1) * rows + (first_t + s) % ((near - 1) * rows)
        return turned(white[at : at + 1])

    earlier = [
        turned(white[top : top + 1]) for top in (first_t - 1, (near - 1) * rows + first_t - 1)
    ]
    toeplitz = []
    for s in range(t_frames):
        tiles = []
        for c in range(2):
            now = frame(c, s)
            tiles += [jnp.where(r, p, q) for r, p, q in zip(rights, now, earlier[c])]
            earlier[c] = now
        toeplitz.append(jnp.concatenate(tiles, axis=0))

    low_half = lax.broadcasted_iota(jnp.int32, (8, LANES), 0) < 4
    low_phase = lax.broadcasted_iota(jnp.int32, (8, LANES), 0) % 4 < 2
    after = jnp.where(place == pieces - 1, 0.0, 1.0).astype(F32)
    lane_row = lax.broadcasted_iota(jnp.int32, (LANES, LANES), 0)
    lane_col = lax.broadcasted_iota(jnp.int32, (LANES, LANES), 1)
    upto = (lane_row <= lane_col).astype(BF16)
    sums = jnp.concatenate([upto, jnp.ones((LANES, LANES), BF16)], axis=1)

    def conv(k):
        crossed = slots[k][1]
        parts = []
        for c in (crossed, 1 - crossed):
            ref, start = piece(c, k)
            top = start + tms * spec_rows + (c ^ crossed) * lag_rows
            parts.append(ref[top : top + lag_rows])
        return jnp.concatenate(parts, axis=1)

    def convolved(members):
        count = len(members)
        filt = [conv(d) for d in members]
        f_all = jnp.concatenate(
            [f[top : top + 16] for top in range(0, lag_rows, 16) for f in filt], axis=0
        )
        accs = [[None] * (out_frames + 1) for _ in members]
        for s in range(0, t_frames, 2):
            both = range(s, min(s + 2, t_frames))
            valid = [
                (a, t, t - (lags - 2) + 2 * a)
                for a in range(lags // 2)
                for t in both
                if 0 <= t - (lags - 2) + 2 * a <= out_frames
            ]
            low = min(a for a, _, _ in valid) // 2
            top = max(a for a, _, _ in valid) // 2 + 1
            g = jnp.dot(
                f_all[low * 16 * count : top * 16 * count],
                jnp.concatenate([toeplitz[t] for t in both], axis=1),
                preferred_element_type=F32,
            )
            for a, t, n in valid:
                for k in range(count):
                    row = ((a // 2 - low) * count + k) * 16 + a % 2 * 8
                    tile = g[row : row + 8, (t - s) * LANES : (t - s + 1) * LANES]
                    accs[k][n] = tile if accs[k][n] is None else accs[k][n] + tile
        return [
            [acc[n + 1] + pltpu.roll(acc[n], 4, 0) for n in range(out_frames)] for acc in accs
        ]

    def outputs(pair, z, corr, power, run):
        lag_now = jnp.where(low_half, lag[pair[0]], lag[pair[1]])
        for n in range(rows):
            tile = slice(8 * n, 8 * n + 8)
            c_re = jnp.where(low_half, corr[0][tile, :LANES], corr[1][tile, :LANES])
            c_im = jnp.where(low_half, corr[0][tile, LANES:], corr[1][tile, LANES:])
            mid = z[n + 1]
            turned = jnp.where(low_phase, -pltpu.roll(mid, 6, 0), pltpu.roll(mid, 2, 0))
            cross = mid * c_re + turned * c_im
            cross = cross + pltpu.roll(cross, 6, 0)
            here = slice(8 * n + 8, 8 * n + 16)
            after_it = slice(8 * n + 16, 8 * n + 24)
            win = (run[tile, LANES:] - run[tile, :LANES] + power[n]) + (
                run[here, LANES:] + run[after_it, :LANES]
            )
            energy = power[n + 1]
            chi = (win - 2.0 * cross + energy * lag_now) / (2 * window + 1)
            lanes = slice(n * LANES, (n + 1) * LANES)
            for top, member in zip((0, 4), pair):
                snr_out[member, :, lanes] = energy[top : top + 2]
                chi_out[member, :, lanes] = chi[top : top + 2]

    dims = (((1,), (1,)), ((), ()))
    for group in range(0, banks, 4):
        members = range(group, min(group + 4, banks))
        frames = convolved(members)
        z_all, power_all, pairs, corr_all = [], [], [], []
        for first in range(0, len(members), 2):
            pairs.append([bank ^ slots[k][0] for k in members[first : first + 2]])
            z0, z1 = frames[first], frames[first + 1]
            z = [jnp.where(low_half, p, pltpu.roll(q, 4, 0)) for p, q in zip(z0, z1)]
            z[-1] = z[-1] * after
            z_all.append(z)
        for z, pair in zip(z_all, pairs):
            stacked = jnp.concatenate(
                [jnp.concatenate(z[n : n + rows], axis=0) for n in range(3)], axis=1
            )
            up, low = split_two(stacked)
            both = jnp.concatenate([up, low], axis=0)
            count = up.shape[0]
            corr = []
            for member in pair:
                b_up = jnp.concatenate([band_up[member, d] for d in range(3)], axis=1)
                b_low = jnp.concatenate([band_low[member, d] for d in range(3)], axis=1)
                one = lax.dot_general(both, b_up, dims, preferred_element_type=F32)
                two = lax.dot_general(up, b_low, dims, preferred_element_type=F32)
                corr.append(one[:count] + one[count:] + two)
            corr_all.append(corr)
            squares = [v * v for v in z]
            power_all.append([v + pltpu.roll(v, 6, 0) for v in squares])
        stacked = jnp.concatenate([v for power in power_all for v in power], axis=0)
        up, low = split_two(stacked)
        run_all = jnp.dot(
            jnp.concatenate([up, low], axis=0), sums, preferred_element_type=F32
        )
        count = stacked.shape[0]
        run_all = run_all[:count] + run_all[count:]
        step = 8 * out_frames
        for k, pair in enumerate(pairs):
            run = run_all[k * step : (k + 1) * step]
            outputs(pair, z_all[k], corr_all[k], power_all[k], run)


ON_CHIP_BYTES = 3 * 2**20


def on_chip(*arrays):
    if sum(a.size * a.dtype.itemsize for a in arrays) > ON_CHIP_BYTES:
        return arrays
    return [pltpu.with_memory_space_constraint(a, pltpu.VMEM) for a in map(jnp.asarray, arrays)]


def on_chip_shape(shape, dtype):
    if 2 * math.prod(shape) * jnp.dtype(dtype).itemsize > ON_CHIP_BYTES:
        return jax.ShapeDtypeStruct(shape, dtype)
    return pltpu.VMEM(shape, dtype)


VMEM = pl.BlockSpec(memory_space=pltpu.VMEM)
SMEM = pl.BlockSpec(memory_space=pltpu.SMEM)


def body(
    strain, gate_mask, psd_reset, psd_ref, psd_rate, filters, basis_count, mixing, autocorrelation
):
    length = strain.shape[1]
    rows = length // LANES
    high = length // 2 // LANES
    banks = lax.axis_size("bank")
    tms = lax.axis_size("tm")
    basis, taps = filters.shape[2:]
    templ = mixing.shape[2]
    window = autocorrelation.shape[2] // 2
    lags = taps // LANES
    outer, shift, start, full = tables(length)

    spec, levels = pl.pallas_call(
        spectrum_kernel,
        out_shape=(
            pltpu.VMEM((4 * high, LANES), BF16),
            pltpu.VMEM((2 * high, LANES), F32),
        ),
        in_specs=[VMEM, VMEM, SMEM] + [VMEM] * 5,
        out_specs=(VMEM, VMEM),
        name="spectrum",
    )(
        strain.reshape(rows, LANES),
        gate_mask.reshape(rows, LANES),
        psd_reset,
        psd_ref.reshape(high, LANES),
        psd_rate.reshape(high, LANES),
        outer,
        shift,
        start,
    )
    combined = pl.pallas_call(
        filter_kernel,
        out_shape=pltpu.VMEM((2 * templ * lags, LANES), BF16),
        in_specs=[VMEM, VMEM, SMEM],
        out_specs=VMEM,
        name="filters",
    )(filters.reshape(basis, taps), mixing.reshape(2 * templ, basis), basis_count)
    distance = 1
    while distance < tms:
        spec = jnp.concatenate([spec, swapped(spec, "tm", distance)])
        distance *= 2
    held = jnp.concatenate([spec, combined])
    slots = [(0, 0)]
    distance = banks // 2
    while distance > 2:
        held = jnp.concatenate([held, swapped(held, "bank", distance)])
        slots = slots + [(d ^ distance, p ^ 1) for d, p in slots]
        distance //= 2
    far = swapped(held, "bank", 2)
    near = swapped(held, "bank", 1)
    first = jnp.concatenate([held, near])
    levels_other = swapped_cores(levels)
    last = swapped(far, "bank", 1)
    second = jnp.concatenate([far, last])
    slots = slots + [(d ^ 1, p ^ 1) for d, p in slots]
    slots = slots + [(d ^ 2, p ^ 1) for d, p in slots]
    first_other = swapped_cores(first)
    second_other = swapped_cores(second)

    band = on_chip_shape((banks, 3, 2 * LANES, LANES), BF16)
    band_up, band_low, lag, levels = pl.pallas_call(
        band_kernel,
        out_shape=(
            band,
            band,
            pltpu.VMEM((banks, 8, LANES), F32),
            pltpu.VMEM((2, 3, 2 * high, LANES), F32),
        ),
        in_specs=[VMEM] * 3,
        out_specs=(VMEM,) * 4,
        name="bands",
    )(autocorrelation, *on_chip(levels, levels_other))

    behind = -(-(taps + window) // length)
    near = behind + 2
    share = templ // 2
    out = jax.ShapeDtypeStruct((banks, share, length), F32)
    return pl.pallas_call(
        functools.partial(
            output_kernel, slots=slots, tms=tms, length=length, taps=taps, window=window
        ),
        out_shape=(out, out),
        in_specs=[VMEM] * 10,
        out_specs=(VMEM, VMEM),
        scratch_shapes=[
            pltpu.VMEM((2, banks * tms + behind + 1, 2 * high, LANES), F32),
            pltpu.VMEM((2, banks * tms, 2 * high, LANES), F32),
            pltpu.VMEM((2, banks * tms, 2 * high, LANES), F32),
            pltpu.VMEM((2, banks * tms + behind + 1, 2 * high, LANES), F32),
        ],
        name="outputs",
    )(*on_chip(first, second, first_other, second_other, full, outer, band_up, band_low, lag, levels))


def solution(mesh):
    return jax.shard_map(
        body,
        mesh=mesh,
        in_specs=(
            P("rate", ("parts", "bank", "tm")),
            P(("parts", "bank", "tm")),
            P(("parts", "bank", "tm")),
            P("rate", None),
            P("rate", None),
            P("bank", "rate", None, None),
            P("bank"),
            P("bank", "rate", None, None, None),
            P(),
        ),
        out_specs=(
            P(None, "rate", ("parts", "bank", "tm")),
            P(None, "rate", ("parts", "bank", "tm")),
        ),
        check_vma=False,
    )
```

```python
import functools
import math

import jax
import jax.numpy as jnp
import numpy as np
from jax import lax
from jax.experimental import pallas as pl
from jax.experimental.pallas import tpu as pltpu
from jax.sharding import PartitionSpec as P


LANES = 128
F32 = jnp.float32
BF16 = jnp.bfloat16


def swapped(block, axis, distance):
    count = lax.axis_size("rate")
    places = range(lax.axis_size(axis) * count)
    route = [(i, (i // count ^ distance) * count + (i % count ^ 1)) for i in places]
    return lax.ppermute(block, (axis, "rate"), route)


def swapped_cores(block):
    return lax.ppermute(block, "rate", [(i, i ^ 1) for i in range(lax.axis_size("rate"))])


def two_terms(table):
    upper = table.astype(BF16)
    return upper, (table - upper.astype(np.float32)).astype(BF16)


def tables(length):
    rows = length // LANES
    high = length // 2 // LANES
    lane = np.arange(LANES)
    turn = 2.0 * math.pi
    outer = turn * (np.arange(rows)[:, None] * lane[None, :] % rows) / rows
    outer = np.stack([np.cos(outer), np.sin(outer)])
    shift = turn * (np.arange(high)[:, None] * lane[None, :] % rows) / rows
    shift = np.stack([np.cos(shift), np.sin(shift)])
    step = 8
    fine = turn * (np.arange(step)[:, None] * lane[None, :]) / length
    coarse = turn * (np.arange(0, LANES, step)[:, None] * lane[None, :]) / length
    start = np.concatenate([np.cos(fine), np.sin(fine), np.cos(coarse), np.sin(coarse)])
    bins = np.arange(length // 2)
    full = turn * (bins[:, None] * lane[None, :] % length) / length
    full = np.concatenate([np.cos(full), np.sin(full)], axis=0)
    outer, shift, start, full = (a.astype(np.float32) for a in (outer, shift, start, full))
    return outer, shift, start, np.concatenate(two_terms(full), axis=1)


def split_two(value):
    upper = value.astype(BF16)
    return upper, (value - upper.astype(F32)).astype(BF16)


def product_two(left, right):
    upper, lower = split_two(left)
    count, width = left.shape[0], right.shape[1] // 2
    both = jnp.dot(jnp.concatenate([upper, lower], axis=0), right, preferred_element_type=F32)
    small = (both[:count, width:] + both[count:, width:]) + both[count:, :width]
    return both[:count, :width] + small


def circulant(row):
    return pltpu.roll(jnp.broadcast_to(row, (LANES, LANES)), 0, 1, stride=1, stride_axis=0)


def keep_right():
    u = lax.broadcasted_iota(jnp.int32, (LANES, LANES), 0)
    q = lax.broadcasted_iota(jnp.int32, (LANES, LANES), 1)
    return q >= u


def spectrum_kernel(strain, mask, reset, psd_ref, psd_rate, outer, shift, start, out, levels):
    rows = strain.shape[0]
    high = psd_ref.shape[0]
    levels[:high] = psd_ref[...]
    levels[high:] = psd_rate[...]
    signal = strain[...] * mask[...].astype(F32)
    step = start.shape[0] // 2 - LANES // 8
    fine_c, fine_s = start[:step], start[step : 2 * step]
    wide_c, wide_s = start[2 * step : 2 * step + LANES // 8], start[2 * step + LANES // 8 :]
    cos_rows, sin_rows = [], []
    for a in range(LANES // 8):
        c, s = wide_c[a : a + 1], wide_s[a : a + 1]
        cos_rows.append(c * fine_c - s * fine_s)
        sin_rows.append(s * fine_c + c * fine_s)
    cos_all, sin_all = jnp.concatenate(cos_rows, axis=0), jnp.concatenate(sin_rows, axis=0)
    terms = [split_two(v) for v in (cos_all, sin_all)]
    inner = jnp.concatenate([terms[0][0], terms[1][0], terms[0][1], terms[1][1]], axis=1)
    left = [signal * shift[i, k : k + 1] for i in range(2) for k in range(high)]
    product = product_two(jnp.concatenate(left, axis=0), inner)
    cos_one, sin_one = outer[0], outer[1]
    real_rows, imag_rows = [], []
    for kh in range(high):
        with_cos = product[kh * rows : (kh + 1) * rows]
        with_sin = product[(high + kh) * rows : (high + kh + 1) * rows]
        cos_sum = with_cos[:, :LANES] - with_sin[:, LANES:]
        sin_sum = with_cos[:, LANES:] + with_sin[:, :LANES]
        real_rows.append(jnp.sum(cos_one * cos_sum - sin_one * sin_sum, axis=0, keepdims=True))
        imag_rows.append(jnp.sum(sin_one * cos_sum + cos_one * sin_sum, axis=0, keepdims=True))
    real_part = jnp.concatenate(real_rows, axis=0)
    imag_part = jnp.concatenate(imag_rows, axis=0)
    row = lax.broadcasted_iota(jnp.int32, imag_part.shape, 0)
    lane = lax.broadcasted_iota(jnp.int32, imag_part.shape, 1)
    imag_part = jnp.where(row + lane == 0, reset[0].astype(F32), imag_part)
    upper, lower = split_two(jnp.concatenate([real_part, imag_part], axis=0))
    out[: 2 * high] = upper
    out[2 * high :] = lower


def filter_kernel(filters, mixing, count, out):
    total, basis = mixing.shape
    share = total // 2
    templ = share // 2
    rate = lax.axis_index("rate")
    row = lax.broadcasted_iota(jnp.int32, (total, total), 0)
    col = lax.broadcasted_iota(jnp.int32, (total, total), 1)
    part = (row // share) ^ rate
    source = (part * templ + row % templ) * 2 + row % share // templ
    choose = (col == source).astype(BF16)
    ordered = jnp.dot(choose, mixing[...], preferred_element_type=F32)
    live = lax.broadcasted_iota(jnp.int32, (total, basis), 1) < count[0]
    ordered = jnp.where(live, ordered, 0.0).astype(BF16)
    combined = jnp.dot(ordered, filters[...], preferred_element_type=F32)
    lags = filters.shape[1] // LANES
    low_half = lax.broadcasted_iota(jnp.int32, (total, LANES), 0) < share
    own, other = [], []
    for a in range(0, lags, 2):
        even = combined[:, a * LANES : (a + 1) * LANES]
        odd = combined[:, (a + 1) * LANES : (a + 2) * LANES]
        own.append(jnp.where(low_half, even, pltpu.roll(odd, share, 0)))
        other.append(jnp.where(low_half, pltpu.roll(even, share, 0), odd))
    out[...] = jnp.concatenate(own + other, axis=0).astype(BF16)


def band_kernel(series, levels, levels_other, upper_out, lower_out, lag_out, levels_out):
    high = levels.shape[0] // 2
    for c, ref in enumerate((levels, levels_other)):
        reference_psd, rate = ref[:high], ref[high:]
        for k, value in enumerate((0.1 * reference_psd, jnp.log(reference_psd), rate)):
            levels_out[c, k] = jnp.concatenate([value, value], axis=0)
    right = keep_right()
    for b in range(series.shape[0]):
        lag = jnp.zeros((1, 1), F32)
        for part in range(2):
            row = series[b, part : part + 1, :]
            lag = lag + jnp.sum(row * row, axis=1, keepdims=True)
            fill = jnp.zeros((1, 3 * LANES - row.shape[1]), F32)
            row = jnp.concatenate([row, fill], axis=1)
            before = jnp.zeros((LANES, LANES), F32)
            for d in range(3):
                now = circulant(row[:, d * LANES : (d + 1) * LANES])
                upper, lower = split_two(jnp.where(right, now, before))
                upper_out[b, d, part * LANES : (part + 1) * LANES] = upper
                lower_out[b, d, part * LANES : (part + 1) * LANES] = lower
                before = now
        lag_out[b] = jnp.broadcast_to(lag, (8, LANES))


def output_kernel(
    own_a, own_b, other_a, other_b, full, outer, band_up, band_low, lag, levels,
    snr_out, chi_out, spec, drives, keeps, logs, *, slots, tms, length, taps, window,
):
    rows = length // LANES
    high = length // 2 // LANES
    spec_rows = 4 * high
    lags = taps // LANES
    lag_rows = lags * 4
    piece_rows = tms * spec_rows + 2 * lag_rows
    pieces = len(slots) * tms
    behind = -(-(taps + window) // length)
    near = behind + 2
    banks = len(slots)
    whole = banks - banks // 4
    bank = lax.axis_index("bank")
    tm = lax.axis_index("tm")
    place = bank * tms + tm
    bufs = ((own_a, own_b), (other_a, other_b))

    def piece(c, d):
        return bufs[c][d // whole], d % whole * piece_rows

    tile_row = lax.broadcasted_iota(jnp.int32, (2 * high, LANES), 0)
    tile_lane = lax.broadcasted_iota(jnp.int32, (2 * high, LANES), 1)
    flag_place = (tile_row == high) & (tile_lane == 0)
    zero = jnp.zeros((2 * high, LANES), F32)
    for c in range(2):
        for i in range(behind):
            spec[c, i] = zero
            logs[c, i] = zero
        spec[c, pieces + behind] = zero
        logs[c, pieces + behind] = zero
        for k, (d, crossed) in enumerate(slots):
            ref, start = piece(c, k)
            for e in range(tms):
                top = start + e * spec_rows
                value = ref[top : top + 2 * high].astype(F32)
                value = value + ref[top + 2 * high : top + 4 * high].astype(F32)
                band = c ^ crossed ^ (e.bit_count() & 1)
                at = (bank ^ d) * tms + (tm ^ e)
                flag = value[high : high + 1, 0:1]
                value = jnp.where(flag_place, 0.0, value)
                square = value * value
                power = (square + pltpu.roll(square, high, 0)) / (length / 2)
                rate = levels[band, 2]
                spec[band, at + behind] = value
                drives[band, at] = rate * jnp.log(power + levels[band, 0])
                keeps[band, at] = (1.0 - rate) * (1.0 - 0.5 * flag)

    def advance(g, states):
        nexts = []
        for c in range(2):
            nexts.append(keeps[c, g] * states[c] + drives[c, g])
            logs[c, g + behind] = nexts[c]
        return tuple(nexts)

    states = (levels[0, 1], levels[1, 1])
    if pieces <= 16:
        for g in range(pieces):
            states = advance(g, states)
    else:
        lax.fori_loop(0, pieces, advance, states)

    cos_one, sin_one = outer[0], outer[1]
    first_bin = (tile_row % high == 0) & (tile_lane == 0)
    weight = jnp.where(first_bin, 1.0 / length, 2.0 / length).astype(F32)
    top_row = lax.broadcasted_iota(jnp.int32, (rows, LANES), 0) == 0
    left = []
    for c in range(2):
        real, imag = [], []
        for i in range(near):
            scaled = spec[c, place + i] * (jnp.exp(-0.5 * logs[c, place + i]) * weight)
            real.append(scaled[:high])
            imag.append(scaled[high:])
        for i in range(near - 1):
            cos_parts, sin_parts = [], []
            for kh in range(high):
                re = jnp.broadcast_to(real[i][kh : kh + 1], (rows, LANES))
                im = jnp.broadcast_to(imag[i][kh : kh + 1], (rows, LANES))
                if i == 0:
                    re = jnp.where(top_row, real[near - 1][kh : kh + 1], re)
                    im = jnp.where(top_row, imag[near - 1][kh : kh + 1], im)
                cos_parts.append(re * cos_one + im * sin_one)
                sin_parts.append(im * cos_one - re * sin_one)
            left.append(jnp.concatenate(cos_parts + sin_parts, axis=1))
    white = product_two(jnp.concatenate(left, axis=0), full[...])
    white = white.astype(BF16).astype(F32)

    first_out = behind * rows - 1
    out_frames = rows + 2
    first_t = first_out - (lags - 1)
    t_frames = lags - 1 + out_frames
    assert first_t == rows and first_t + t_frames - 1 == (near - 1) * rows
    step = 16
    u_row = lax.broadcasted_iota(jnp.int32, (step, LANES), 0)
    q_lane = lax.broadcasted_iota(jnp.int32, (step, LANES), 1)
    rights = [q_lane >= u_row + top for top in range(0, LANES, step)]

    def turned(row):
        whole = circulant(row).astype(BF16)
        return [whole[top : top + step] for top in range(0, LANES, step)]

    def frame(c, s):
        at = c * (near - 1) * rows + (first_t + s) % ((near - 1) * rows)
        return turned(white[at : at + 1])

    earlier = [
        turned(white[top : top + 1]) for top in (first_t - 1, (near - 1) * rows + first_t - 1)
    ]
    toeplitz = []
    for s in range(t_frames):
        tiles = []
        for c in range(2):
            now = frame(c, s)
            tiles += [jnp.where(r, p, q) for r, p, q in zip(rights, now, earlier[c])]
            earlier[c] = now
        toeplitz.append(jnp.concatenate(tiles, axis=0))

    low_half = lax.broadcasted_iota(jnp.int32, (8, LANES), 0) < 4
    low_phase = lax.broadcasted_iota(jnp.int32, (8, LANES), 0) % 4 < 2
    after = jnp.where(place == pieces - 1, 0.0, 1.0).astype(F32)
    lane_row = lax.broadcasted_iota(jnp.int32, (LANES, LANES), 0)
    lane_col = lax.broadcasted_iota(jnp.int32, (LANES, LANES), 1)
    upto = (lane_row <= lane_col).astype(BF16)
    sums = jnp.concatenate([upto, jnp.ones((LANES, LANES), BF16)], axis=1)

    def conv(k):
        crossed = slots[k][1]
        parts = []
        for c in (crossed, 1 - crossed):
            ref, start = piece(c, k)
            top = start + tms * spec_rows + (c ^ crossed) * lag_rows
            parts.append(ref[top : top + lag_rows])
        return jnp.concatenate(parts, axis=1)

    def convolved(members):
        count = len(members)
        filt = [conv(d) for d in members]
        f_all = jnp.concatenate(
            [f[top : top + 16] for top in range(0, lag_rows, 16) for f in filt], axis=0
        )
        accs = [[None] * (out_frames + 1) for _ in members]
        for s in range(0, t_frames, 2):
            both = range(s, min(s + 2, t_frames))
            valid = [
                (a, t, t - (lags - 2) + 2 * a)
                for a in range(lags // 2)
                for t in both
                if 0 <= t - (lags - 2) + 2 * a <= out_frames
            ]
            low = min(a for a, _, _ in valid) // 2
            top = max(a for a, _, _ in valid) // 2 + 1
            g = jnp.dot(
                f_all[low * 16 * count : top * 16 * count],
                jnp.concatenate([toeplitz[t] for t in both], axis=1),
                preferred_element_type=F32,
            )
            for a, t, n in valid:
                for k in range(count):
                    row = ((a // 2 - low) * count + k) * 16 + a % 2 * 8
                    tile = g[row : row + 8, (t - s) * LANES : (t - s + 1) * LANES]
                    accs[k][n] = tile if accs[k][n] is None else accs[k][n] + tile
        return [
            [acc[n + 1] + pltpu.roll(acc[n], 4, 0) for n in range(out_frames)] for acc in accs
        ]

    def outputs(pair, z, corr, power, run):
        lag_now = jnp.where(low_half, lag[pair[0]], lag[pair[1]])
        for n in range(rows):
            tile = slice(8 * n, 8 * n + 8)
            c_re = jnp.where(low_half, corr[0][tile, :LANES], corr[1][tile, :LANES])
            c_im = jnp.where(low_half, corr[0][tile, LANES:], corr[1][tile, LANES:])
            mid = z[n + 1]
            turned = jnp.where(low_phase, -pltpu.roll(mid, 6, 0), pltpu.roll(mid, 2, 0))
            cross = mid * c_re + turned * c_im
            cross = cross + pltpu.roll(cross, 6, 0)
            here = slice(8 * n + 8, 8 * n + 16)
            after_it = slice(8 * n + 16, 8 * n + 24)
            win = (run[tile, LANES:] - run[tile, :LANES] + power[n]) + (
                run[here, LANES:] + run[after_it, :LANES]
            )
            energy = power[n + 1]
            chi = (win - 2.0 * cross + energy * lag_now) / (2 * window + 1)
            lanes = slice(n * LANES, (n + 1) * LANES)
            for top, member in zip((0, 4), pair):
                snr_out[member, :, lanes] = energy[top : top + 2]
                chi_out[member, :, lanes] = chi[top : top + 2]

    dims = (((1,), (1,)), ((), ()))
    for group in range(0, banks, 4):
        members = range(group, min(group + 4, banks))
        frames = convolved(members)
        z_all, power_all, pairs, corr_all = [], [], [], []
        for first in range(0, len(members), 2):
            pairs.append([bank ^ slots[k][0] for k in members[first : first + 2]])
            z0, z1 = frames[first], frames[first + 1]
            z = [jnp.where(low_half, p, pltpu.roll(q, 4, 0)) for p, q in zip(z0, z1)]
            z[-1] = z[-1] * after
            z_all.append(z)
        for z, pair in zip(z_all, pairs):
            stacked = jnp.concatenate(
                [jnp.concatenate(z[n : n + rows], axis=0) for n in range(3)], axis=1
            )
            up, low = split_two(stacked)
            both = jnp.concatenate([up, low], axis=0)
            count = up.shape[0]
            corr = []
            for member in pair:
                b_up = jnp.concatenate([band_up[member, d] for d in range(3)], axis=1)
                b_low = jnp.concatenate([band_low[member, d] for d in range(3)], axis=1)
                one = lax.dot_general(both, b_up, dims, preferred_element_type=F32)
                two = lax.dot_general(up, b_low, dims, preferred_element_type=F32)
                corr.append(one[:count] + one[count:] + two)
            corr_all.append(corr)
            squares = [v * v for v in z]
            power_all.append([v + pltpu.roll(v, 6, 0) for v in squares])
        stacked = jnp.concatenate([v for power in power_all for v in power], axis=0)
        up, low = split_two(stacked)
        run_all = jnp.dot(
            jnp.concatenate([up, low], axis=0), sums, preferred_element_type=F32
        )
        count = stacked.shape[0]
        run_all = run_all[:count] + run_all[count:]
        step = 8 * out_frames
        for k, pair in enumerate(pairs):
            run = run_all[k * step : (k + 1) * step]
            outputs(pair, z_all[k], corr_all[k], power_all[k], run)


ON_CHIP_BYTES = 3 * 2**20


def on_chip(*arrays):
    if sum(a.size * a.dtype.itemsize for a in arrays) > ON_CHIP_BYTES:
        return arrays
    return [pltpu.with_memory_space_constraint(a, pltpu.VMEM) for a in map(jnp.asarray, arrays)]


def on_chip_shape(shape, dtype):
    if 2 * math.prod(shape) * jnp.dtype(dtype).itemsize > ON_CHIP_BYTES:
        return jax.ShapeDtypeStruct(shape, dtype)
    return pltpu.VMEM(shape, dtype)


VMEM = pl.BlockSpec(memory_space=pltpu.VMEM)
SMEM = pl.BlockSpec(memory_space=pltpu.SMEM)


def body(
    strain, gate_mask, psd_reset, psd_ref, psd_rate, filters, basis_count, mixing, autocorrelation
):
    length = strain.shape[1]
    rows = length // LANES
    high = length // 2 // LANES
    banks = lax.axis_size("bank")
    tms = lax.axis_size("tm")
    basis, taps = filters.shape[2:]
    templ = mixing.shape[2]
    window = autocorrelation.shape[2] // 2
    lags = taps // LANES
    outer, shift, start, full = tables(length)

    spec, levels = pl.pallas_call(
        spectrum_kernel,
        out_shape=(
            pltpu.VMEM((4 * high, LANES), BF16),
            pltpu.VMEM((2 * high, LANES), F32),
        ),
        in_specs=[VMEM, VMEM, SMEM] + [VMEM] * 5,
        out_specs=(VMEM, VMEM),
        name="spectrum",
    )(
        strain.reshape(rows, LANES),
        gate_mask.reshape(rows, LANES),
        psd_reset,
        psd_ref.reshape(high, LANES),
        psd_rate.reshape(high, LANES),
        outer,
        shift,
        start,
    )
    combined = pl.pallas_call(
        filter_kernel,
        out_shape=pltpu.VMEM((2 * templ * lags, LANES), BF16),
        in_specs=[VMEM, VMEM, SMEM],
        out_specs=VMEM,
        name="filters",
    )(filters.reshape(basis, taps), mixing.reshape(2 * templ, basis), basis_count)
    distance = 1
    while distance < tms:
        spec = jnp.concatenate([spec, swapped(spec, "tm", distance)])
        distance *= 2
    held = jnp.concatenate([spec, combined])
    slots = [(0, 0)]
    distance = banks // 2
    while distance > 2:
        held = jnp.concatenate([held, swapped(held, "bank", distance)])
        slots = slots + [(d ^ distance, p ^ 1) for d, p in slots]
        distance //= 2
    far = swapped(held, "bank", 2)
    near = swapped(held, "bank", 1)
    levels_other = swapped_cores(levels)
    last = swapped(far, "bank", 1)
    early = jnp.concatenate([held, near, far])
    slots = slots + [(d ^ 1, p ^ 1) for d, p in slots]
    slots = slots + [(d ^ 2, p ^ 1) for d, p in slots]
    early_other = swapped_cores(early)
    last_other = swapped_cores(last)

    band = on_chip_shape((banks, 3, 2 * LANES, LANES), BF16)
    band_up, band_low, lag, levels = pl.pallas_call(
        band_kernel,
        out_shape=(
            band,
            band,
            pltpu.VMEM((banks, 8, LANES), F32),
            pltpu.VMEM((2, 3, 2 * high, LANES), F32),
        ),
        in_specs=[VMEM] * 3,
        out_specs=(VMEM,) * 4,
        name="bands",
    )(autocorrelation, *on_chip(levels, levels_other))

    behind = -(-(taps + window) // length)
    near = behind + 2
    share = templ // 2
    out = jax.ShapeDtypeStruct((banks, share, length), F32)
    return pl.pallas_call(
        functools.partial(
            output_kernel, slots=slots, tms=tms, length=length, taps=taps, window=window
        ),
        out_shape=(out, out),
        in_specs=[VMEM] * 10,
        out_specs=(VMEM, VMEM),
        scratch_shapes=[
            pltpu.VMEM((2, banks * tms + behind + 1, 2 * high, LANES), F32),
            pltpu.VMEM((2, banks * tms, 2 * high, LANES), F32),
            pltpu.VMEM((2, banks * tms, 2 * high, LANES), F32),
            pltpu.VMEM((2, banks * tms + behind + 1, 2 * high, LANES), F32),
        ],
        name="outputs",
    )(*on_chip(early, last, early_other, last_other, full, outer, band_up, band_low, lag, levels))


def solution(mesh):
    return jax.shard_map(
        body,
        mesh=mesh,
        in_specs=(
            P("rate", ("parts", "bank", "tm")),
            P(("parts", "bank", "tm")),
            P(("parts", "bank", "tm")),
            P("rate", None),
            P("rate", None),
            P("bank", "rate", None, None),
            P("bank"),
            P("bank", "rate", None, None, None),
            P(),
        ),
        out_specs=(
            P(None, "rate", ("parts", "bank", "tm")),
            P(None, "rate", ("parts", "bank", "tm")),
        ),
        check_vma=False,
    )
```
